32 devices in a mesh: dp: 16 (over z, x, core), tensor: 2 (over y).
Axes of the slice: x: 2, y: 2, z: 4, core: 2. Of those that a mesh axis runs over, the one named last changes fastest.
Arguments:
- tokens_in: float32 [16384, 1536], P(('dp', 'tensor')), may hold values from -6 to 6
- prefix_len: int32 [16], P('dp'), may hold values from 102 to 512
- attn_gain: float32 [1536], replicated, may hold values from 0.1 to 1.9
- query_weight: bfloat16 [1536, 1536], P(None, 'tensor'), may hold values from -0.15625 to 0.15625
- key_weight: bfloat16 [1536, 1536], P(None, 'tensor'), may hold values from -0.15625 to 0.15625
- value_weight: bfloat16 [1536, 1536], P(None, 'tensor'), may hold values from -0.15625 to 0.15625
- forget_weight: bfloat16 [1536, 24], P(None, 'tensor'), may hold values from -0.15625 to 0.15625
- forget_bias: float32 [24], P('tensor'), may hold values from 1.5 to 7
- outgate_weight: bfloat16 [1536, 1536], P(None, 'tensor'), may hold values from -0.15625 to 0.15625
- output_weight: bfloat16 [1536, 1536], P('tensor'), may hold values from -0.625 to 0.625
- mlp_gain: float32 [1536], replicated, may hold values from 0.1 to 1.9
- gate_weight: bfloat16 [1536, 4096], P(None, 'tensor'), may hold values from -0.15625 to 0.15625
- up_weight: bfloat16 [1536, 4096], P(None, 'tensor'), may hold values from -0.15625 to 0.15625
- down_weight: bfloat16 [4096, 1536], P('tensor'), may hold values from -0.09375 to 0.09375
- out_grad: float32 [16384, 1536], P(('dp', 'tensor')), may hold values from -6 to 6
Outputs:
- layer_out: float32 [16384, 1536], P(('dp', 'tensor'))
- input_grad: float32 [16384, 1536], P(('dp', 'tensor'))
- attn_gain_grad: float32 [1536], replicated
- query_grad: float32 [1536, 1536], P('dp', 'tensor')
- key_grad: float32 [1536, 1536], P('dp', 'tensor')
- value_grad: float32 [1536, 1536], P('dp', 'tensor')
- forget_grad: float32 [1536, 24], P('dp', 'tensor')
- bias_grad: float32 [24], replicated
- outgate_grad: float32 [1536, 1536], P('dp', 'tensor')
- output_grad: float32 [1536, 1536], P('tensor', 'dp')
- mlp_gain_grad: float32 [1536], replicated
- gate_grad: float32 [1536, 4096], P('dp', 'tensor')
- up_grad: float32 [1536, 4096], P('dp', 'tensor')
- down_grad: float32 [4096, 1536], P('tensor', 'dp')
The draws below stay inside these ranges and needn't reach their ends.
Inputs may be any that keep to these rules, and one draw needn't show every extreme that they name: `prefix_len`: one prefix length for each sequence, drawn independently.
All inputs are finite; a program needn't handle non-finite values.
Results may differ from the reference program's by a relative error of at most 0.025.
Values may be sent and summed in bfloat16 or wider, within the bound.
A program may use at most 320 MiB of HBM per device.

```python
import jax
import jax.numpy as jnp
from jax import lax

D = 1536
H = 24
HD = 64
FF = 4096
LEN = 1024
NSEQ = 16
TOKENS = 16384


def plant(result, rng, least, high):
    dims = result.shape
    index_at = [jax.random.randint(jax.random.fold_in(rng, axis), (), 0, dims[axis]) for axis in range(len(dims))]
    result = result.at[tuple(index_at)].set(least)
    longest = dims.index(max(dims))
    index_at[longest] = (index_at[longest] + 1) % dims[longest]
    return result.at[tuple(index_at)].set(high)


def with_spikes(values, stream_key, source, target, shards_of, factor):
    def block_of(position):
        return (jnp.arange(values.shape[position]) // (values.shape[position] // shards_of)).reshape((-1,) + (1,) * (values.ndim - 1 - position))

    one_side = jax.random.permutation(stream_key, shards_of)[block_of(target)]
    other_side = (block_of(target) + shards_of // 2) % shards_of
    return jnp.where((block_of(source) == one_side) | (block_of(source) == other_side), factor * values, values)


def block_levels(rng, dims, split, least, high):
    factor_of, own = 1.0, jax.random.fold_in(rng, 6)
    for position, shards_of in split:
        draws = jnp.exp(jax.random.uniform(jax.random.fold_in(own, position), (shards_of,), jnp.float32, least / len(split), high / len(split)))
        factor_of = factor_of * jnp.repeat(draws, dims[position] // shards_of).reshape([-1 if axis == position else 1 for axis in range(len(dims))])
    return factor_of


def noise(rng, extent, scale, bound, pieces=(), dtype=jnp.bfloat16):
    entries = scale * jax.random.normal(rng, extent, jnp.float32)
    if pieces:
        entries = entries * block_levels(rng, extent, pieces, -0.22, 0.18)
    return jnp.clip(entries, -bound, bound).astype(dtype)


def gaussian_with(key, extent, deviation, bound, pieces, heavy, kind=jnp.bfloat16):
    values = deviation * jax.random.normal(key, extent, jnp.float32)
    if pieces:
        values = values * block_levels(key, extent, pieces, -0.22, 0.18)
    return jnp.clip(with_spikes(values, jax.random.fold_in(key, 3), *heavy), -bound, bound).astype(kind)


def setup_inputs(seed: int = 0) -> dict:
    key_of = jax.random.split(jax.random.key(seed), 16)
    return {
        "tokens_in": gaussian_with(key_of[0], (TOKENS, D), 1.0, 6.0, ((0, 32),), (0, 1, 32, 2.75), jnp.float32),
        "prefix_len": plant(jax.random.randint(key_of[1], (NSEQ,), LEN // 10, LEN // 2 + 1), jax.random.fold_in(key_of[1], 1), LEN // 10, (LEN // 2 + 1) - 1).astype(jnp.int32),
        "attn_gain": jnp.clip(1.0 + 0.18 * jax.random.normal(key_of[2], (D,), jnp.float32), 0.1, 1.9),
        "query_weight": noise(key_of[3], (D, D), D ** -0.5, 0.15625, ((1, 2),)),
        "key_weight": noise(key_of[4], (D, D), D ** -0.5, 0.15625, ((1, 2),)),
        "value_weight": noise(key_of[5], (D, D), D ** -0.5, 0.15625, ((1, 2),)),
        "forget_weight": noise(key_of[6], (D, H), D ** -0.5, 0.15625, ((1, 2),)),
        "forget_bias": jnp.clip(1.5 + 5.5 * jax.random.uniform(key_of[7], (H,), jnp.float32) ** block_levels(key_of[7], (H,), ((0, 2),), -0.2, 0.2), 1.5, 7.0),
        "outgate_weight": noise(key_of[8], (D, D), D ** -0.5, 0.15625, ((1, 2),)),
        "output_weight": noise(key_of[9], (D, D), (D // 16) ** -0.5, 0.625, ((0, 2),)),
        "mlp_gain": jnp.clip(1.0 + 0.18 * jax.random.normal(key_of[10], (D,), jnp.float32), 0.1, 1.9),
        "gate_weight": noise(key_of[11], (D, FF), D ** -0.5, 0.15625, ((1, 2),)),
        "up_weight": noise(key_of[12], (D, FF), D ** -0.5, 0.15625, ((1, 2),)),
        "down_weight": noise(key_of[13], (FF, D), FF ** -0.5, 0.09375, ((0, 2),)),
        "out_grad": gaussian_with(key_of[14], (TOKENS, D), 1.0, 6.0, ((0, 32),), (0, 1, 32, 2.75), jnp.float32),
    }


epsilon = 1e-06
highest = lax.Precision.HIGHEST

@jax.custom_vjp
def low(v):
    return lax.optimization_barrier(v.astype(jnp.bfloat16)).astype(jnp.float32)

@jax.custom_vjp
def low_back(v):
    return v

def low_keep(v):
    return (low(v), None)

def low_pass(kept, grad):
    return (grad,)

def back_keep(v):
    return (v, None)

def back_low(kept, grad):
    return (low(grad),)
low.defvjp(low_keep, low_pass)
low_back.defvjp(back_keep, back_low)

def matmul(left, right):
    return jnp.dot(left, right, precision=highest)

def rms_scale(rows, gain):
    return rows * lax.rsqrt(lax.optimization_barrier(jnp.mean(rows * rows, axis=-1, keepdims=True)) + epsilon) * gain

def attend_head(query_h, key_h, value_h, decay_h, prefix_size):
    positions = jnp.arange(LEN)
    causal = positions[None, :] <= positions[:, None]
    allowed = causal | (positions[:, None] < prefix_size) & (positions[None, :] < prefix_size)
    decay_gap = decay_h[:, None] - decay_h[None, :]
    raw_scores = matmul(query_h, key_h.T) * HD ** (-0.5) + jnp.where(causal, decay_gap, -decay_gap)
    scores = jnp.where(allowed, low_back(raw_scores), -1e+30)
    log_total = jax.nn.logsumexp(scores, axis=-1, keepdims=True)
    attn_probs = jnp.exp(scores - log_total)
    return low_back(matmul(low(attn_probs), value_h))

def heads_first(array):
    return array.reshape(LEN, H, HD).transpose(1, 0, 2)

def layer_sequence(params, rows, prefix_size):
    attn_gain, query_weight, key_weight, value_weight, forget_weight, forget_bias, outgate_weight, output_weight, mlp_gain, gate_weight, up_weight, down_weight = params
    normed = low(rms_scale(rows, attn_gain))
    queries = low_back(low(matmul(normed, query_weight)))
    keys_all = low_back(low(matmul(normed, key_weight)))
    values_all = low_back(low(matmul(normed, value_weight)))
    forget_logit = low_back(matmul(normed, forget_weight) + forget_bias)
    decay = jnp.cumsum(jax.nn.log_sigmoid(forget_logit), axis=0)
    outgate = jax.nn.sigmoid(low_back(matmul(normed, outgate_weight)))

    def per_head(slices):
        return attend_head(slices[0], slices[1], slices[2], slices[3], prefix_size)
    attended = lax.map(jax.checkpoint(per_head), (heads_first(queries), heads_first(keys_all), heads_first(values_all), decay.T))
    attended = attended.transpose(1, 0, 2).reshape(LEN, D)
    mixed = low_back(low(outgate * attended))
    hidden = rows + low_back(matmul(mixed, output_weight))
    normed_two = low(rms_scale(hidden, mlp_gain))
    gate = low_back(matmul(normed_two, gate_weight))
    upward = low_back(matmul(normed_two, up_weight))
    active = low_back(low(jax.nn.silu(gate) * upward))
    return hidden + low_back(matmul(active, down_weight))

def reference(tokens_in, prefix_len, attn_gain, query_weight, key_weight, value_weight, forget_weight, forget_bias, outgate_weight, output_weight, mlp_gain, gate_weight, up_weight, down_weight, out_grad):
    params = tuple((array.astype(jnp.float32) for array in (attn_gain, query_weight, key_weight, value_weight, forget_weight, forget_bias, outgate_weight, output_weight, mlp_gain, gate_weight, up_weight, down_weight)))
    number = prefix_len.shape[0]

    def whole(weights, inputs):

        def advance(state, slices):
            return (state, jax.checkpoint(layer_sequence)(weights, slices[0], slices[1]))
        _, outputs = lax.scan(advance, jnp.zeros((), jnp.float32), (inputs.reshape(number, LEN, D), prefix_len))
        return outputs.reshape(number * LEN, D)
    layer_out, pull = jax.vjp(whole, params, tokens_in.astype(jnp.float32))
    grads, input_grad = pull(out_grad.astype(jnp.float32))
    return (layer_out, input_grad, grads[0], grads[1], grads[2], grads[3], grads[4], grads[5], grads[6], grads[7], grads[8], grads[9], grads[10], grads[11])
```

```python
import jax
import jax.numpy as jnp
from jax import lax
from jax.experimental import pallas as pl
from jax.experimental.pallas import tpu as pltpu
from jax.sharding import PartitionSpec as P

H = 24
HD = 64
LEN = 1024
LANES = 128
FAR = -1e30


epsilon = 1e-06


def dot_nn(left, right):
    return lax.dot_general(
        left, right, (((1,), (0,)), ((), ())), preferred_element_type=jnp.float32
    )


def dot_nt(left, right):
    return lax.dot_general(
        left, right, (((1,), (1,)), ((), ())), preferred_element_type=jnp.float32
    )


def dot_tn(left, right):
    return lax.dot_general(
        left, right, (((0,), (0,)), ((), ())), preferred_element_type=jnp.float32
    )


def lane_of(shape, head):
    lane = lax.broadcasted_iota(jnp.int32, shape, 1)
    return lane - (1 - head) * HD, (lane // HD) == head


def three_lanes(relative, first, column, otherwise):
    high = column.astype(jnp.bfloat16).astype(jnp.float32)
    rest = column - high
    middle = rest.astype(jnp.bfloat16).astype(jnp.float32)
    low = rest - middle
    placed = jnp.where(relative == first + 2, low, otherwise)
    placed = jnp.where(relative == first + 1, middle, placed)
    return jnp.where(relative == first, high, placed)


def lanes_at(relative, first, value, otherwise):
    return jnp.where((relative >= first) & (relative < first + 3), value, otherwise)


def quarters(ref):
    return [ref.at[:, part * LANES : (part + 1) * LANES] for part in range(4)]


def forward_kernel(where_ref, qkvz_ref, d_ref, mixed_ref, att_ref, total_ref, qa, qu, ka):
    q_ref, k_ref, v_ref, z_ref = quarters(qkvz_ref)
    length = q_ref.shape[0]
    half, quarter = length // 2, length // 4
    prefix, first, second = where_ref[0], where_ref[1], where_ref[2]
    first = pl.multiple_of(first, half)
    second = pl.multiple_of(second, half)
    early = pl.ds(first, half)
    for head in range(2):
        relative, own = lane_of((length, LANES), head)
        decay = jnp.broadcast_to(d_ref[0, :, head : head + 1], (length, LANES))
        plus = three_lanes(relative, 0, decay, lanes_at(relative, 3, 1.0, 0.0))
        minus = three_lanes(relative, 3, -decay, lanes_at(relative, 0, 1.0, 0.0))
        scaled = q_ref[...].astype(jnp.float32) * HD**-0.5
        qa[...] = jnp.where(own, scaled, plus).astype(jnp.bfloat16)
        qu[...] = jnp.where(own, scaled, -plus).astype(jnp.bfloat16)
        ka[...] = jnp.where(own, k_ref[...].astype(jnp.float32), minus).astype(jnp.bfloat16)
        lanes = slice(head * HD, head * HD + HD)

        def finish(rows, parts, lanes=lanes, head=head):
            top = parts[0][0].max(axis=1, keepdims=True)
            for scores, _ in parts[1:]:
                top = jnp.maximum(top, scores.max(axis=1, keepdims=True))
            norm, out = 0.0, 0.0
            for scores, keys in parts:
                weight = jnp.exp(scores - top)
                norm = norm + weight.sum(axis=1, keepdims=True)
                out = out + dot_nn(weight.astype(jnp.bfloat16), v_ref[keys, :])
            att_ref[rows, lanes] = (out / norm)[:, lanes]
            total_ref[0, rows, head : head + 1] = top + jnp.log(norm)

        for part in range(2):
            rows = pl.ds(first + part * quarter, quarter)
            i = lax.broadcasted_iota(jnp.int32, (quarter, half), 0) + part * quarter
            j = lax.broadcasted_iota(jnp.int32, (quarter, half), 1)
            both = (i < prefix) & (j < prefix)
            below = dot_nt(qa[rows, :], ka[early, :])
            above = dot_nt(qu[rows, :], ka[early, :])
            scores = jnp.where(j <= i, below, jnp.where(both, above, FAR))
            finish(rows, [(scores, early)])
        for part in range(2):
            rows = pl.ds(second + part * quarter, quarter)
            width = (part + 1) * quarter
            late = pl.ds(second, width)
            i = lax.broadcasted_iota(jnp.int32, (quarter, width), 0) + part * quarter
            j = lax.broadcasted_iota(jnp.int32, (quarter, width), 1)
            finish(
                rows,
                [
                    (dot_nt(qa[rows, :], ka[early, :]), early),
                    (jnp.where(j <= i, dot_nt(qa[rows, :], ka[late, :]), FAR), late),
                ],
            )
    mixed_ref[...] = (jax.nn.sigmoid(z_ref[...].astype(jnp.float32)) * att_ref[...]).astype(
        jnp.bfloat16
    )


def backward_kernel(
    where_ref,
    qkvz_ref,
    gm_ref,
    att_ref,
    d_ref,
    total_ref,
    grads_ref,
    gd_ref,
    qa,
    qu,
    ka,
    va,
    ga,
    acc_q,
    acc_k,
    acc_v,
):
    q_ref, k_ref, v_ref, z_ref = quarters(qkvz_ref)
    dq_ref, dk_ref, dv_ref, dz_ref = quarters(grads_ref)
    length = q_ref.shape[0]
    half, quarter = length // 2, length // 4
    prefix, first, second = where_ref[0], where_ref[1], where_ref[2]
    first = pl.multiple_of(first, half)
    second = pl.multiple_of(second, half)
    outgate = jax.nn.sigmoid(z_ref[...].astype(jnp.float32))
    grad_mixed = gm_ref[...].astype(jnp.float32)
    attended = att_ref[...]
    grad_att = (grad_mixed * outgate).astype(jnp.bfloat16).astype(jnp.float32)
    dz_ref[...] = (grad_mixed * attended * outgate * (1.0 - outgate)).astype(jnp.bfloat16)
    product = grad_att * attended
    for head in range(2):
        relative, own = lane_of((length, LANES), head)
        delta = jnp.sum(jnp.where(own, product, 0.0), axis=1, keepdims=True)
        delta = jnp.broadcast_to(delta, (length, LANES))
        decay = jnp.broadcast_to(d_ref[0, :, head : head + 1], (length, LANES))
        total = jnp.broadcast_to(total_ref[0, :, head : head + 1], (length, LANES))
        ones = lanes_at(relative, 3, 1.0, 0.0)
        ones_front = lanes_at(relative, 0, 1.0, 0.0)
        scaled = q_ref[...].astype(jnp.float32) * HD**-0.5
        qa[...] = jnp.where(own, scaled, three_lanes(relative, 0, decay - total, ones)).astype(
            jnp.bfloat16
        )
        qu[...] = jnp.where(own, scaled, three_lanes(relative, 0, -decay - total, -ones)).astype(
            jnp.bfloat16
        )
        ka[...] = jnp.where(
            own, k_ref[...].astype(jnp.float32), three_lanes(relative, 3, -decay, ones_front)
        ).astype(jnp.bfloat16)
        va[...] = jnp.where(own, v_ref[...].astype(jnp.float32), ones_front).astype(jnp.bfloat16)
        ga[...] = jnp.where(own, grad_att, three_lanes(relative, 0, -delta, 0.0)).astype(
            jnp.bfloat16
        )
        lanes = slice(head * HD, head * HD + HD)
        free = (1 - head) * HD

        def unit(keys, queries, shape, key_start, query_start, prefixed, masked, fresh_k, fresh_q,
                 head=head):
            score = dot_nt(ka[keys, :], qa[queries, :])
            if prefixed or masked:
                j = lax.broadcasted_iota(jnp.int32, shape, 0) + key_start
                i = lax.broadcasted_iota(jnp.int32, shape, 1) + query_start
                causal = j <= i
                other = FAR
                if prefixed:
                    above = dot_nt(ka[keys, :], qu[queries, :])
                    other = jnp.where((i < prefix) & (j < prefix), above, FAR)
                score = jnp.where(causal, score, other)
            probs = jnp.exp(score)
            grad = (probs * dot_nt(va[keys, :], ga[queries, :])).astype(jnp.bfloat16)
            part_v = dot_nn(probs.astype(jnp.bfloat16), ga[queries, :])
            part_k = dot_nn(grad, qa[queries, :])
            part_q = dot_tn(grad, ka[keys, :])
            if prefixed:
                turned = jnp.where(causal, 0.0, -2.0 * grad.astype(jnp.float32)).astype(
                    jnp.bfloat16
                )
                back_k, _ = lane_of((shape[1], LANES), head)
                back_q, _ = lane_of((shape[0], LANES), head)
                part_k = part_k + dot_nn(turned, jnp.where(back_k == 3, 1.0, 0.0).astype(jnp.bfloat16))
                part_q = part_q + dot_tn(turned, jnp.where(back_q == 0, 1.0, 0.0).astype(jnp.bfloat16))
            if fresh_k:
                acc_k[keys, :] = part_k
                acc_v[keys, :] = part_v
            else:
                acc_k[keys, :] += part_k
                acc_v[keys, :] += part_v
            if fresh_q:
                acc_q[queries, :] = part_q
            else:
                acc_q[queries, :] += part_q

        early = pl.ds(first, half)
        for part in range(2):
            queries = pl.ds(first + part * quarter, quarter)
            unit(early, queries, (half, quarter), 0, part * quarter, True, False, part == 0, True)
        for part in range(2):
            queries = pl.ds(second + part * quarter, quarter)
            unit(early, queries, (half, quarter), 0, 0, False, False, False, True)
        unit(pl.ds(second, half), pl.ds(second + quarter, quarter), (half, quarter), 0, quarter,
             False, True, True, False)
        unit(pl.ds(second, quarter), pl.ds(second, quarter), (quarter, quarter), 0, 0,
             False, True, False, False)
        dq_ref[:, lanes] = (acc_q[:, lanes] * HD**-0.5).astype(jnp.bfloat16)
        dk_ref[:, lanes] = acc_k[:, lanes].astype(jnp.bfloat16)
        dv_ref[:, lanes] = acc_v[:, lanes].astype(jnp.bfloat16)
        gd_ref[0, :, head : head + 1] = acc_q[:, free : free + 1] - acc_k[:, free + 3 : free + 4]


def wide(length, columns, offset=0):
    return pl.BlockSpec((length, columns), lambda pair, where: (0, pair + offset))


def narrow(length, offset=0):
    return pl.BlockSpec((1, length, 2), lambda pair, where: (pair + offset, 0, 0))


def attention_forward(places, qkvz, decay):
    length = qkvz.shape[0]
    pairs = decay.shape[0]
    return pl.pallas_call(
        forward_kernel,
        grid_spec=pltpu.PrefetchScalarGridSpec(
            num_scalar_prefetch=1,
            grid=(pairs,),
            in_specs=[wide(length, 4 * LANES), narrow(length)],
            out_specs=[wide(length, LANES)] * 2 + [narrow(length)],
            scratch_shapes=[pltpu.VMEM((length, LANES), jnp.bfloat16)] * 3,
        ),
        out_shape=[
            jax.ShapeDtypeStruct((length, pairs * LANES), jnp.bfloat16),
            jax.ShapeDtypeStruct((length, pairs * LANES), jnp.float32),
            jax.ShapeDtypeStruct((pairs, length, 2), jnp.float32),
        ],
        compiler_params=pltpu.CompilerParams(vmem_limit_bytes=56 << 20),
        cost_estimate=pl.CostEstimate(
            flops=pairs * 5_000_000_000, bytes_accessed=15_000_000, transcendentals=0
        ),
        name="attention_forward",
    )(places, qkvz, decay)


def attention_backward(places, qkvz, grad_mixed, attended, decay, log_total, start, count):
    length = qkvz.shape[0]
    return pl.pallas_call(
        backward_kernel,
        grid_spec=pltpu.PrefetchScalarGridSpec(
            num_scalar_prefetch=1,
            grid=(count,),
            in_specs=[wide(length, 4 * LANES, start)]
            + [wide(length, LANES, start)] * 2
            + [narrow(length, start)] * 2,
            out_specs=[wide(length, 4 * LANES), narrow(length)],
            scratch_shapes=[pltpu.VMEM((length, LANES), jnp.bfloat16)] * 5
            + [pltpu.VMEM((length, LANES), jnp.float32)] * 3,
        ),
        out_shape=[
            jax.ShapeDtypeStruct((length, count * 4 * LANES), jnp.bfloat16),
            jax.ShapeDtypeStruct((count, length, 2), jnp.float32),
        ],
        compiler_params=pltpu.CompilerParams(vmem_limit_bytes=56 << 20),
        cost_estimate=pl.CostEstimate(
            flops=count * 8_000_000_000, bytes_accessed=15_000_000, transcendentals=0
        ),
        name="attention_backward",
    )(places, qkvz, grad_mixed, attended, decay, log_total)


def weight_term(left, right):
    return lax.dot_general(
        left, right, (((0,), (0,)), ((), ())), preferred_element_type=jnp.float32
    )


def rms_rows(rows, gain):
    inverse = lax.rsqrt(jnp.mean(rows * rows, axis=-1, keepdims=True) + epsilon)
    return (inverse, rows * inverse * gain)


def rms_back(rows, inverse, gain, grad):
    scaled = grad * gain
    gain_term = jnp.sum(grad * rows * inverse, axis=0)
    row_term = inverse * scaled - rows * inverse**3 * jnp.mean(
        scaled * rows, axis=-1, keepdims=True
    )
    return (row_term, gain_term)


def tie(*values):
    return lax.optimization_barrier(values)


def swap(rows):
    return lax.ppermute(rows, "tensor", [(0, 1), (1, 0)])


def two_devices():
    return lax.axis_size("tensor") == 2


def gather_rows(rows, other=None):
    if not two_devices():
        return lax.all_gather(rows, "tensor", axis=0, tiled=True)
    return jnp.concatenate([rows, swap(rows) if other is None else other], axis=0)


def half_starts(length):
    if not two_devices():
        return jnp.array(0, jnp.int32), jnp.array(length // 2, jnp.int32)
    first = lax.axis_index("tensor") * (length // 2)
    return first, length // 2 - first


def scatter_rows(product, length):
    if not two_devices():
        return lax.psum_scatter(
            product(0, length).astype(jnp.bfloat16), "tensor", scatter_dimension=0, tiled=True
        ).astype(jnp.float32), 0.0
    sent = product(length // 2, length).astype(jnp.bfloat16)
    arrived = swap(sent)
    _, start = tie(sent, jnp.zeros((), jnp.float32))
    return product(0, length // 2), arrived


class WeightSum:
    def __init__(self, partial, masks):
        self.size = lax.axis_size("dp")
        bits = self.size.bit_length() - 1
        rows, columns = partial.shape
        self.terms = [
            partial.astype(jnp.bfloat16).reshape((2,) * bits + (rows // self.size, columns))
        ]
        self.left = list(range(bits - 1, -1, -1))
        self.masks = list(masks)

    def send(self, critical):
        if not self.masks:
            return critical
        mask = self.masks.pop(0)
        bit = mask.bit_length() - 1
        axis = self.left.index(bit)
        self.left.remove(bit)
        mine = (lax.axis_index("dp") // mask) % 2
        sent = sum(
            lax.dynamic_index_in_dim(term, 1 - mine, axis, False).astype(jnp.float32)
            for term in self.terms
        ).astype(jnp.bfloat16)
        critical, sent = tie(critical, sent)
        arrived = lax.ppermute(sent, "dp", [(i, i ^ mask) for i in range(self.size)])
        self.terms = [
            lax.dynamic_index_in_dim(term, mine, axis, False) for term in self.terms
        ] + [arrived]
        return critical

    def arrive(self, critical):
        critical, self.terms[-1] = tie(critical, self.terms[-1])
        return critical

    def result(self):
        while self.masks:
            self.send(jnp.zeros((), jnp.float32))
        return sum(term.astype(jnp.float32) for term in self.terms)


def all_sum(value):
    size = lax.axis_size("dp")
    mask = 1
    while mask < size:
        value = value + lax.ppermute(value, "dp", [(i, i ^ mask) for i in range(size)])
        mask *= 2
    if not two_devices():
        return lax.psum(value, "tensor")
    return value + swap(value)


def pair_columns(weights, pairs):
    width = pairs * LANES
    padded = [jnp.pad(w, ((0, 0), (0, width - w.shape[1]))) for w in weights]
    parts = [w[:, p * LANES : (p + 1) * LANES] for p in range(pairs) for w in padded]
    return jnp.concatenate(parts, axis=1)


def running_sum(order, values):
    high = lax.reduce_precision(values, 8, 7)
    middle = lax.reduce_precision(values - high, 8, 7)
    terms = jnp.concatenate([high, middle, values - high - middle], axis=1).astype(jnp.bfloat16)
    sums = dot_nn(order, terms)
    return sum(jnp.split(sums, 3, axis=1))


def by_pairs(columns):
    length, heads = columns.shape
    columns = jnp.pad(columns, ((0, 0), (0, heads % 2)))
    return columns.reshape(length, -1, 2).transpose(1, 0, 2)


def from_pairs(pairs, heads):
    return pairs.transpose(1, 0, 2).reshape(pairs.shape[1], -1)[:, :heads]


def local(
    tokens_in,
    prefix_len,
    attn_gain,
    query_weight,
    key_weight,
    value_weight,
    forget_weight,
    forget_bias,
    outgate_weight,
    output_weight,
    mlp_gain,
    gate_weight,
    up_weight,
    down_weight,
    out_grad,
):
    heads_here = forget_weight.shape[1]
    assert prefix_len.shape[0] == 1
    pairs = (heads_here + 1) // 2
    width = heads_here * HD
    first, second = half_starts(LEN)
    places = jnp.stack([prefix_len[0], first, second])
    index = jnp.arange(LEN, dtype=jnp.int32)
    position = (index + first) % LEN
    earlier = (position[None, :] <= position[:, None]).astype(jnp.bfloat16)
    later = (position[None, :] >= position[:, None]).astype(jnp.bfloat16)
    bits = lax.axis_size("dp").bit_length() - 1
    near = [1 << bit for bit in range(bits)]
    far = near[:1] + near[2:] + near[1:2]

    scale_one, normed_rows = rms_rows(tokens_in, attn_gain)
    normed = gather_rows(normed_rows.astype(jnp.bfloat16))
    projection = pair_columns((query_weight, key_weight, value_weight, outgate_weight), pairs)
    output_padded = jnp.pad(output_weight, ((0, pairs * LANES - width), (0, 0)))
    normed, branch_rows = tie(normed, out_grad.astype(jnp.bfloat16))
    grad_branch = gather_rows(branch_rows)
    qkvz = dot_nn(normed, projection).astype(jnp.bfloat16)
    forget_logit = dot_nn(normed, forget_weight) + forget_bias
    decay = by_pairs(running_sum(earlier, jax.nn.log_sigmoid(forget_logit)))
    mixed, attended, log_total = attention_forward(places, qkvz, decay)
    mixed, grad_branch = tie(mixed, grad_branch)
    own, arrived = scatter_rows(lambda a, b: dot_nn(mixed[a:b], output_padded), LEN)
    grad_active = dot_nt(grad_branch, down_weight).astype(jnp.bfloat16)
    own, grad_active = tie(own, grad_active)
    hidden_rows = tokens_in + (own + arrived)

    scale_two, normed_two_rows = rms_rows(hidden_rows, mlp_gain)
    normed_two = gather_rows(normed_two_rows.astype(jnp.bfloat16))
    gate = dot_nn(normed_two, gate_weight)
    upward = dot_nn(normed_two, up_weight)
    active = (jax.nn.silu(gate) * upward).astype(jnp.bfloat16)
    gate_sigmoid = jax.nn.sigmoid(gate)
    grad_act_f = grad_active.astype(jnp.float32)
    grad_gate = (grad_act_f * upward * gate_sigmoid * (1.0 + gate * (1.0 - gate_sigmoid))).astype(
        jnp.bfloat16
    )
    grad_upward = (grad_act_f * gate * gate_sigmoid).astype(jnp.bfloat16)
    own, arrived = scatter_rows(
        lambda a, b: dot_nt(grad_gate[a:b], gate_weight) + dot_nt(grad_upward[a:b], up_weight), LEN
    )
    own, grad_branch, active = tie(own, grad_branch, active)
    down = WeightSum(weight_term(grad_branch, active), near)
    own = down.send(own)
    own, normed_two = tie(own, normed_two)
    gate_sum = WeightSum(weight_term(normed_two, grad_gate), near)
    own = gate_sum.send(own)
    own = down.arrive(own)
    own = down.send(own)
    grad_normed_two = own + arrived
    grad_hidden, mlp_gain_part = rms_back(hidden_rows, scale_two, mlp_gain, grad_normed_two)
    grad_hidden = grad_hidden + out_grad
    mid_rows = grad_hidden.astype(jnp.bfloat16)
    mid_rows, normed_two, active = tie(mid_rows, normed_two, active)
    other = swap(mid_rows) if two_devices() else jnp.zeros((), jnp.float32)
    up_sum = WeightSum(weight_term(normed_two, grad_upward), near)
    other = up_sum.send(other)
    other = gate_sum.arrive(other)
    other = gate_sum.send(other)
    last_own, last_arrived = scatter_rows(lambda a, b: dot_nn(active[a:b], down_weight), LEN)
    other, last_own = tie(other, last_own)
    other = up_sum.arrive(other)
    other = up_sum.send(other)
    grad_mid = gather_rows(mid_rows, other)

    grad_mixed = dot_nt(grad_mid, output_padded).astype(jnp.bfloat16)
    grad_mixed = down.arrive(grad_mixed)
    grad_mixed = down.send(grad_mixed)
    cut = pairs // 2
    saved = (attended, decay, log_total)
    grads_a, decay_a = attention_backward(places, qkvz, grad_mixed, *saved, 0, cut)
    grads_a, mixed, grad_mid = tie(grads_a, mixed, grad_mid)
    output_sum = WeightSum(weight_term(grad_mid, mixed)[:, :width], far)
    grads_a = output_sum.send(grads_a)
    grads_a = down.arrive(grads_a)
    grads_a = down.send(grads_a)
    grads_a = gate_sum.arrive(grads_a)
    grads_a = gate_sum.send(grads_a)
    grads_a, grad_mixed = tie(grads_a, grad_mixed)
    sum_a = WeightSum(weight_term(normed, grads_a), far)
    grad_mixed = sum_a.send(grad_mixed)
    grad_mixed = output_sum.arrive(grad_mixed)
    grad_mixed = output_sum.send(grad_mixed)
    grad_mixed, last_arrived = tie(grad_mixed, last_arrived)
    layer_out = hidden_rows + (last_own + last_arrived)
    grads_b, decay_b = attention_backward(places, qkvz, grad_mixed, *saved, cut, pairs - cut)
    for each in (down, gate_sum, up_sum, sum_a, output_sum):
        grads_b = each.arrive(grads_b)
        grads_b = each.send(grads_b)
    grad_decay = from_pairs(jnp.concatenate([decay_a, decay_b], axis=0), heads_here)
    grad_forget = (running_sum(later, grad_decay) * jax.nn.sigmoid(-forget_logit)).astype(
        jnp.bfloat16
    )
    bias_part = jnp.sum(grad_forget.astype(jnp.float32), axis=0)
    middle = cut * 4 * LANES

    def normed_term(a, b):
        term = dot_nt(grads_a[a:b], projection[:, :middle])
        term = term + dot_nt(grads_b[a:b], projection[:, middle:])
        return term + dot_nt(grad_forget[a:b], forget_weight)

    own, arrived = scatter_rows(normed_term, LEN)
    own, normed = tie(own, normed)
    sum_b = WeightSum(weight_term(normed, grads_b), near)
    own = sum_b.send(own)
    forget_sum = WeightSum(weight_term(normed, grad_forget), far)
    own = forget_sum.send(own)
    own = sum_b.arrive(own)
    own = sum_b.send(own)
    grad_normed = own + arrived
    input_part, attn_gain_part = rms_back(tokens_in, scale_one, attn_gain, grad_normed)
    input_grad = grad_hidden + input_part

    down_grad = down.result().T
    gate_grad = gate_sum.result()
    up_grad = up_sum.result()
    output_grad = output_sum.result().T
    forget_grad = forget_sum.result()
    block = jnp.concatenate([sum_a.result(), sum_b.result()], axis=1)
    block = block.reshape(block.shape[0], pairs, 4, LANES)
    query_grad, key_grad, value_grad, outgate_grad = [
        block[:, :, part].reshape(block.shape[0], pairs * LANES)[:, :width] for part in range(4)
    ]
    bias_full = lax.dynamic_update_slice_in_dim(
        jnp.zeros((H,), jnp.float32), bias_part, lax.axis_index("tensor") * heads_here, 0
    )
    summed = all_sum(jnp.concatenate([attn_gain_part, mlp_gain_part, bias_full]))
    width = attn_gain_part.shape[0]
    attn_gain_grad, mlp_gain_grad, bias_grad = jnp.split(summed, [width, 2 * width])
    return (
        layer_out,
        input_grad,
        attn_gain_grad,
        query_grad,
        key_grad,
        value_grad,
        forget_grad,
        bias_grad,
        outgate_grad,
        output_grad,
        mlp_gain_grad,
        gate_grad,
        up_grad,
        down_grad,
    )


def solution(mesh):
    in_specs = (
        P(("dp", "tensor"), None),
        P("dp"),
        P(),
        P(None, "tensor"),
        P(None, "tensor"),
        P(None, "tensor"),
        P(None, "tensor"),
        P("tensor"),
        P(None, "tensor"),
        P("tensor", None),
        P(),
        P(None, "tensor"),
        P(None, "tensor"),
        P("tensor", None),
        P(("dp", "tensor"), None),
    )
    out_specs = (
        P(("dp", "tensor"), None),
        P(("dp", "tensor"), None),
        P(),
        P("dp", "tensor"),
        P("dp", "tensor"),
        P("dp", "tensor"),
        P("dp", "tensor"),
        P(),
        P("dp", "tensor"),
        P("tensor", "dp"),
        P(),
        P("dp", "tensor"),
        P("dp", "tensor"),
        P("tensor", "dp"),
    )
    return jax.shard_map(local, mesh=mesh, in_specs=in_specs, out_specs=out_specs, check_vma=False)
```

```python
import jax
import jax.numpy as jnp
from jax import lax
from jax.experimental import pallas as pl
from jax.experimental.pallas import tpu as pltpu
from jax.sharding import PartitionSpec as P

H = 24
HD = 64
LEN = 1024
LANES = 128
FAR = -1e30


epsilon = 1e-06


def dot_nn(left, right):
    return lax.dot_general(
        left, right, (((1,), (0,)), ((), ())), preferred_element_type=jnp.float32
    )


def dot_nt(left, right):
    return lax.dot_general(
        left, right, (((1,), (1,)), ((), ())), preferred_element_type=jnp.float32
    )


def dot_tn(left, right):
    return lax.dot_general(
        left, right, (((0,), (0,)), ((), ())), preferred_element_type=jnp.float32
    )


def lane_of(shape, head):
    lane = lax.broadcasted_iota(jnp.int32, shape, 1)
    return lane - (1 - head) * HD, (lane // HD) == head


def three_lanes(relative, first, column, otherwise):
    high = column.astype(jnp.bfloat16).astype(jnp.float32)
    rest = column - high
    middle = rest.astype(jnp.bfloat16).astype(jnp.float32)
    low = rest - middle
    placed = jnp.where(relative == first + 2, low, otherwise)
    placed = jnp.where(relative == first + 1, middle, placed)
    return jnp.where(relative == first, high, placed)


def lanes_at(relative, first, value, otherwise):
    return jnp.where((relative >= first) & (relative < first + 3), value, otherwise)


def quarters(ref):
    return [ref.at[:, part * LANES : (part + 1) * LANES] for part in range(4)]


def forward_kernel(where_ref, qkvz_ref, d_ref, mixed_ref, att_ref, total_ref, qa, qu, ka):
    q_ref, k_ref, v_ref, z_ref = quarters(qkvz_ref)
    length = q_ref.shape[0]
    half, quarter = length // 2, length // 4
    prefix, first, second = where_ref[0], where_ref[1], where_ref[2]
    first = pl.multiple_of(first, half)
    second = pl.multiple_of(second, half)
    early = pl.ds(first, half)
    for head in range(2):
        relative, own = lane_of((length, LANES), head)
        decay = jnp.broadcast_to(d_ref[0, :, head : head + 1], (length, LANES))
        plus = three_lanes(relative, 0, decay, lanes_at(relative, 3, 1.0, 0.0))
        minus = three_lanes(relative, 3, -decay, lanes_at(relative, 0, 1.0, 0.0))
        scaled = q_ref[...].astype(jnp.float32) * HD**-0.5
        qa[...] = jnp.where(own, scaled, plus).astype(jnp.bfloat16)
        qu[...] = jnp.where(own, scaled, -plus).astype(jnp.bfloat16)
        ka[...] = jnp.where(own, k_ref[...].astype(jnp.float32), minus).astype(jnp.bfloat16)
        lanes = slice(head * HD, head * HD + HD)

        def finish(rows, parts, lanes=lanes, head=head):
            top = parts[0][0].max(axis=1, keepdims=True)
            for scores, _ in parts[1:]:
                top = jnp.maximum(top, scores.max(axis=1, keepdims=True))
            norm, out = 0.0, 0.0
            for scores, keys in parts:
                weight = jnp.exp(scores - top)
                norm = norm + weight.sum(axis=1, keepdims=True)
                out = out + dot_nn(weight.astype(jnp.bfloat16), v_ref[keys, :])
            att_ref[rows, lanes] = (out / norm)[:, lanes]
            total_ref[0, rows, head : head + 1] = top + jnp.log(norm)

        for part in range(2):
            rows = pl.ds(first + part * quarter, quarter)
            i = lax.broadcasted_iota(jnp.int32, (quarter, half), 0) + part * quarter
            j = lax.broadcasted_iota(jnp.int32, (quarter, half), 1)
            both = (i < prefix) & (j < prefix)
            below = dot_nt(qa[rows, :], ka[early, :])
            above = dot_nt(qu[rows, :], ka[early, :])
            scores = jnp.where(j <= i, below, jnp.where(both, above, FAR))
            finish(rows, [(scores, early)])
        for part in range(2):
            rows = pl.ds(second + part * quarter, quarter)
            width = (part + 1) * quarter
            late = pl.ds(second, width)
            i = lax.broadcasted_iota(jnp.int32, (quarter, width), 0) + part * quarter
            j = lax.broadcasted_iota(jnp.int32, (quarter, width), 1)
            finish(
                rows,
                [
                    (dot_nt(qa[rows, :], ka[early, :]), early),
                    (jnp.where(j <= i, dot_nt(qa[rows, :], ka[late, :]), FAR), late),
                ],
            )
    mixed_ref[...] = (jax.nn.sigmoid(z_ref[...].astype(jnp.float32)) * att_ref[...]).astype(
        jnp.bfloat16
    )


def backward_kernel(
    where_ref,
    qkvz_ref,
    gm_ref,
    att_ref,
    d_ref,
    total_ref,
    grads_ref,
    gd_ref,
    qa,
    qu,
    ka,
    va,
    ga,
    acc_q,
    acc_k,
    acc_v,
):
    q_ref, k_ref, v_ref, z_ref = quarters(qkvz_ref)
    dq_ref, dk_ref, dv_ref, dz_ref = quarters(grads_ref)
    length = q_ref.shape[0]
    half, quarter = length // 2, length // 4
    prefix, first, second = where_ref[0], where_ref[1], where_ref[2]
    first = pl.multiple_of(first, half)
    second = pl.multiple_of(second, half)
    outgate = jax.nn.sigmoid(z_ref[...].astype(jnp.float32))
    grad_mixed = gm_ref[...].astype(jnp.float32)
    attended = att_ref[...]
    grad_att = (grad_mixed * outgate).astype(jnp.bfloat16).astype(jnp.float32)
    dz_ref[...] = (grad_mixed * attended * outgate * (1.0 - outgate)).astype(jnp.bfloat16)
    product = grad_att * attended
    for head in range(2):
        relative, own = lane_of((length, LANES), head)
        delta = jnp.sum(jnp.where(own, product, 0.0), axis=1, keepdims=True)
        delta = jnp.broadcast_to(delta, (length, LANES))
        decay = jnp.broadcast_to(d_ref[0, :, head : head + 1], (length, LANES))
        total = jnp.broadcast_to(total_ref[0, :, head : head + 1], (length, LANES))
        ones = lanes_at(relative, 3, 1.0, 0.0)
        ones_front = lanes_at(relative, 0, 1.0, 0.0)
        scaled = q_ref[...].astype(jnp.float32) * HD**-0.5
        qa[...] = jnp.where(own, scaled, three_lanes(relative, 0, decay - total, ones)).astype(
            jnp.bfloat16
        )
        qu[...] = jnp.where(own, scaled, three_lanes(relative, 0, -decay - total, -ones)).astype(
            jnp.bfloat16
        )
        ka[...] = jnp.where(
            own, k_ref[...].astype(jnp.float32), three_lanes(relative, 3, -decay, ones_front)
        ).astype(jnp.bfloat16)
        va[...] = jnp.where(own, v_ref[...].astype(jnp.float32), ones_front).astype(jnp.bfloat16)
        ga[...] = jnp.where(own, grad_att, three_lanes(relative, 0, -delta, 0.0)).astype(
            jnp.bfloat16
        )
        lanes = slice(head * HD, head * HD + HD)
        free = (1 - head) * HD

        def unit(keys, queries, shape, key_start, query_start, prefixed, masked, fresh_k, fresh_q,
                 head=head):
            score = dot_nt(ka[keys, :], qa[queries, :])
            if prefixed or masked:
                j = lax.broadcasted_iota(jnp.int32, shape, 0) + key_start
                i = lax.broadcasted_iota(jnp.int32, shape, 1) + query_start
                causal = j <= i
                other = FAR
                if prefixed:
                    above = dot_nt(ka[keys, :], qu[queries, :])
                    other = jnp.where((i < prefix) & (j < prefix), above, FAR)
                score = jnp.where(causal, score, other)
            probs = jnp.exp(score)
            grad = (probs * dot_nt(va[keys, :], ga[queries, :])).astype(jnp.bfloat16)
            part_v = dot_nn(probs.astype(jnp.bfloat16), ga[queries, :])
            part_k = dot_nn(grad, qa[queries, :])
            part_q = dot_tn(grad, ka[keys, :])
            if prefixed:
                turned = jnp.where(causal, 0.0, -2.0 * grad.astype(jnp.float32)).astype(
                    jnp.bfloat16
                )
                back_k, _ = lane_of((shape[1], LANES), head)
                back_q, _ = lane_of((shape[0], LANES), head)
                part_k = part_k + dot_nn(turned, jnp.where(back_k == 3, 1.0, 0.0).astype(jnp.bfloat16))
                part_q = part_q + dot_tn(turned, jnp.where(back_q == 0, 1.0, 0.0).astype(jnp.bfloat16))
            if fresh_k:
                acc_k[keys, :] = part_k
                acc_v[keys, :] = part_v
            else:
                acc_k[keys, :] += part_k
                acc_v[keys, :] += part_v
            if fresh_q:
                acc_q[queries, :] = part_q
            else:
                acc_q[queries, :] += part_q

        early = pl.ds(first, half)
        for part in range(2):
            queries = pl.ds(first + part * quarter, quarter)
            unit(early, queries, (half, quarter), 0, part * quarter, True, False, part == 0, True)
        for part in range(2):
            queries = pl.ds(second + part * quarter, quarter)
            unit(early, queries, (half, quarter), 0, 0, False, False, False, True)
        unit(pl.ds(second, half), pl.ds(second + quarter, quarter), (half, quarter), 0, quarter,
             False, True, True, False)
        unit(pl.ds(second, quarter), pl.ds(second, quarter), (quarter, quarter), 0, 0,
             False, True, False, False)
        dq_ref[:, lanes] = (acc_q[:, lanes] * HD**-0.5).astype(jnp.bfloat16)
        dk_ref[:, lanes] = acc_k[:, lanes].astype(jnp.bfloat16)
        dv_ref[:, lanes] = acc_v[:, lanes].astype(jnp.bfloat16)
        gd_ref[0, :, head : head + 1] = acc_q[:, free : free + 1] - acc_k[:, free + 3 : free + 4]


def wide(length, columns, offset=0):
    return pl.BlockSpec((length, columns), lambda pair, where: (0, pair + offset))


def narrow(length, offset=0):
    return pl.BlockSpec((1, length, 2), lambda pair, where: (pair + offset, 0, 0))


def attention_forward(places, qkvz, decay):
    length = qkvz.shape[0]
    pairs = decay.shape[0]
    return pl.pallas_call(
        forward_kernel,
        grid_spec=pltpu.PrefetchScalarGridSpec(
            num_scalar_prefetch=1,
            grid=(pairs,),
            in_specs=[wide(length, 4 * LANES), narrow(length)],
            out_specs=[wide(length, LANES)] * 2 + [narrow(length)],
            scratch_shapes=[pltpu.VMEM((length, LANES), jnp.bfloat16)] * 3,
        ),
        out_shape=[
            jax.ShapeDtypeStruct((length, pairs * LANES), jnp.bfloat16),
            jax.ShapeDtypeStruct((length, pairs * LANES), jnp.float32),
            jax.ShapeDtypeStruct((pairs, length, 2), jnp.float32),
        ],
        compiler_params=pltpu.CompilerParams(vmem_limit_bytes=56 << 20),
        cost_estimate=pl.CostEstimate(
            flops=7_000_000_000, bytes_accessed=10_000_000, transcendentals=0
        ),
        name="attention_forward",
    )(places, qkvz, decay)


def attention_backward(places, qkvz, grad_mixed, attended, decay, log_total, start, count):
    length = qkvz.shape[0]
    return pl.pallas_call(
        backward_kernel,
        grid_spec=pltpu.PrefetchScalarGridSpec(
            num_scalar_prefetch=1,
            grid=(count,),
            in_specs=[wide(length, 4 * LANES, start)]
            + [wide(length, LANES, start)] * 2
            + [narrow(length, start)] * 2,
            out_specs=[wide(length, 4 * LANES), narrow(length)],
            scratch_shapes=[pltpu.VMEM((length, LANES), jnp.bfloat16)] * 5
            + [pltpu.VMEM((length, LANES), jnp.float32)] * 3,
        ),
        out_shape=[
            jax.ShapeDtypeStruct((length, count * 4 * LANES), jnp.bfloat16),
            jax.ShapeDtypeStruct((count, length, 2), jnp.float32),
        ],
        compiler_params=pltpu.CompilerParams(vmem_limit_bytes=56 << 20),
        cost_estimate=pl.CostEstimate(
            flops=7_000_000_000, bytes_accessed=10_000_000, transcendentals=0
        ),
        name="attention_backward",
    )(places, qkvz, grad_mixed, attended, decay, log_total)


def weight_term(left, right):
    return lax.dot_general(
        left, right, (((0,), (0,)), ((), ())), preferred_element_type=jnp.float32
    )


def rms_rows(rows, gain):
    inverse = lax.rsqrt(jnp.mean(rows * rows, axis=-1, keepdims=True) + epsilon)
    return (inverse, rows * inverse * gain)


def rms_back(rows, inverse, gain, grad):
    scaled = grad * gain
    gain_term = jnp.sum(grad * rows * inverse, axis=0)
    row_term = inverse * scaled - rows * inverse**3 * jnp.mean(
        scaled * rows, axis=-1, keepdims=True
    )
    return (row_term, gain_term)


def tie(*values):
    return lax.optimization_barrier(values)


def swap(rows):
    return lax.ppermute(rows, "tensor", [(0, 1), (1, 0)])


def two_devices():
    return lax.axis_size("tensor") == 2


def gather_rows(rows, other=None):
    if not two_devices():
        return lax.all_gather(rows, "tensor", axis=0, tiled=True)
    return jnp.concatenate([rows, swap(rows) if other is None else other], axis=0)


def half_starts(length):
    if not two_devices():
        return jnp.array(0, jnp.int32), jnp.array(length // 2, jnp.int32)
    first = lax.axis_index("tensor") * (length // 2)
    return first, length // 2 - first


class Line:
    def __init__(self):
        self.token = jnp.zeros((), jnp.float32)

    def start(self, values):
        self.token, values = tie(self.token, values)
        return values

    def run(self, step, *values):
        return self.start(step(*self.start(values)))


def scatter_rows(line, product, values, length):
    if not two_devices():
        term = line.run(lambda *v: product(0, length, *v).astype(jnp.bfloat16), *values)
        return lax.psum_scatter(term, "tensor", scatter_dimension=0, tiled=True), jnp.zeros(
            (), jnp.bfloat16
        )
    sent = line.run(lambda *v: product(length // 2, length, *v).astype(jnp.bfloat16), *values)
    arrived = swap(sent)
    return line.run(lambda *v: product(0, length // 2, *v), *values), arrived


def halves_kernel(mine_ref, left_ref, right_ref, kept_ref, sent_ref, total):
    total[...] = dot_tn(left_ref[...], right_ref[...])
    count, rows, _ = kept_ref.shape
    mine = mine_ref[0]
    for pair in range(count):
        for ref, place in ((kept_ref, mine), (sent_ref, 1 - mine)):
            start = pl.multiple_of((2 * pair + place) * rows, 8)
            ref[pair] = total[pl.ds(start, rows), :].astype(ref.dtype)


def weight_halves(left, right, size):
    length, rows = left.shape
    columns = right.shape[1]
    step = 384
    block = rows // size
    assert rows % step == 0 and step % (2 * block) == 0
    count = step // (2 * block)
    mine = (lax.axis_index("dp") % 2).reshape(1)
    half = pl.BlockSpec((count, block, columns), lambda i, mine: (i, 0, 0))
    return pl.pallas_call(
        halves_kernel,
        grid_spec=pltpu.PrefetchScalarGridSpec(
            num_scalar_prefetch=1,
            grid=(rows // step,),
            in_specs=[
                pl.BlockSpec((length, step), lambda i, mine: (0, i)),
                pl.BlockSpec((length, columns), lambda i, mine: (0, 0)),
            ],
            out_specs=[half, half],
            scratch_shapes=[pltpu.VMEM((step, columns), jnp.float32)],
        ),
        out_shape=[jax.ShapeDtypeStruct((size // 2, block, columns), jnp.bfloat16)] * 2,
        compiler_params=pltpu.CompilerParams(vmem_limit_bytes=40 << 20),
        cost_estimate=pl.CostEstimate(flops=7_000_000_000, bytes_accessed=10_000_000, transcendentals=0),
        name="weight_halves",
    )(mine, left, right)


class WeightSum:
    def __init__(self, line, left, right, masks):
        self.line = line
        self.size = lax.axis_size("dp")
        self.bits = self.size.bit_length() - 1
        kept, sent = line.run(lambda *v: weight_halves(*v, self.size), left, right)
        shape = (2,) * (self.bits - 1) + kept.shape[1:]
        assert masks[0] == 1
        self.masks = list(masks[1:])
        self.left = list(range(self.bits - 1, 0, -1))
        self.terms = [kept.reshape(shape), self.exchange(sent.reshape(shape), 1)]

    def exchange(self, sent, mask):
        return lax.ppermute(sent, "dp", [(i, i ^ mask) for i in range(self.size)])

    def arrive(self):
        self.terms[-1] = self.line.start(self.terms[-1])

    def step(self):
        if not self.masks:
            return
        mask = self.masks.pop(0)
        axis = self.left.index(mask.bit_length() - 1)
        self.left.remove(mask.bit_length() - 1)
        mine = (lax.axis_index("dp") // mask) % 2
        self.arrive()
        sent = sum(
            lax.dynamic_index_in_dim(term, 1 - mine, axis, False).astype(jnp.float32)
            for term in self.terms
        ).astype(jnp.bfloat16)
        sent = self.line.start(sent)
        arrived = self.exchange(sent, mask)
        self.terms = [
            lax.dynamic_index_in_dim(term, mine, axis, False) for term in self.terms
        ] + [arrived]

    def result(self, finish=lambda total: total):
        while self.masks:
            self.step()
        return self.line.run(
            lambda *terms: finish(sum(term.astype(jnp.float32) for term in terms)), *self.terms
        )


class AllSum:
    def __init__(self, line, value, rows):
        self.line, self.value, self.rows, self.mask = line, value, rows, 1
        self.arrived = jnp.zeros((), value.dtype)
        self.step()

    def step(self):
        size = lax.axis_size("dp")
        if self.mask < size:
            mask = self.mask
            self.value = self.line.run(lambda a, b: a + b, self.value, self.arrived)
            self.arrived = lax.ppermute(self.value, "dp", [(i, i ^ mask) for i in range(size)])
            self.mask *= 2

    def result(self):
        while self.mask < lax.axis_size("dp"):
            self.step()
        value = self.line.run(lambda a, b: a + b, self.value, self.arrived)
        top = value[: self.rows]
        if not two_devices():
            return lax.psum(top, "tensor"), value[self.rows :]
        return self.line.run(lambda a, b: a + b, top, swap(top)), value[self.rows :]


def pair_columns(weights, pairs):
    width = pairs * LANES
    padded = [jnp.pad(w, ((0, 0), (0, width - w.shape[1]))) for w in weights]
    parts = [w[:, p * LANES : (p + 1) * LANES] for p in range(pairs) for w in padded]
    return jnp.concatenate(parts, axis=1)


def running_sum(order, values):
    high = lax.reduce_precision(values, 8, 7)
    middle = lax.reduce_precision(values - high, 8, 7)
    terms = jnp.concatenate([high, middle, values - high - middle], axis=1).astype(jnp.bfloat16)
    sums = dot_nn(order, terms)
    return sum(jnp.split(sums, 3, axis=1))


def by_pairs(columns):
    length, heads = columns.shape
    columns = jnp.pad(columns, ((0, 0), (0, heads % 2)))
    return columns.reshape(length, -1, 2).transpose(1, 0, 2)


def from_pairs(pairs, heads):
    return pairs.transpose(1, 0, 2).reshape(pairs.shape[1], -1)[:, :heads]


def local(
    tokens_in,
    prefix_len,
    attn_gain,
    query_weight,
    key_weight,
    value_weight,
    forget_weight,
    forget_bias,
    outgate_weight,
    output_weight,
    mlp_gain,
    gate_weight,
    up_weight,
    down_weight,
    out_grad,
):
    heads_here = forget_weight.shape[1]
    assert prefix_len.shape[0] == 1
    pairs = (heads_here + 1) // 2
    width = heads_here * HD
    first, second = half_starts(LEN)
    places = jnp.stack([prefix_len[0], first, second])
    index = jnp.arange(LEN, dtype=jnp.int32)
    position = (index + first) % LEN
    earlier = (position[None, :] <= position[:, None]).astype(jnp.bfloat16)
    later = (position[None, :] >= position[:, None]).astype(jnp.bfloat16)
    bits = lax.axis_size("dp").bit_length() - 1
    near = [1 << bit for bit in range(bits)]
    far = near[:1] + near[2:] + near[1:2]

    scale_one, normed_rows = rms_rows(tokens_in, attn_gain)
    normed = gather_rows(normed_rows.astype(jnp.bfloat16))
    projection = pair_columns((query_weight, key_weight, value_weight, outgate_weight), pairs)
    output_padded = jnp.pad(output_weight, ((0, pairs * LANES - width), (0, 0)))
    normed, branch_rows = tie(normed, out_grad.astype(jnp.bfloat16))
    grad_branch = gather_rows(branch_rows)
    qkvz = dot_nn(normed, projection).astype(jnp.bfloat16)
    forget_logit = dot_nn(normed, forget_weight) + forget_bias
    decay = by_pairs(running_sum(earlier, jax.nn.log_sigmoid(forget_logit)))
    mixed, attended, log_total = attention_forward(places, qkvz, decay)
    line = Line()
    own, arrived = scatter_rows(
        line, lambda a, b, m, w: dot_nn(m[a:b], w), (mixed, output_padded), LEN
    )
    grad_active = line.run(
        lambda g, w: dot_nt(g, w).astype(jnp.bfloat16), grad_branch, down_weight
    )
    hidden_rows = tokens_in + line.run(lambda a, b: a + b, own, arrived)

    scale_two, normed_two_rows = rms_rows(hidden_rows, mlp_gain)
    normed_two = gather_rows(normed_two_rows.astype(jnp.bfloat16))

    def gated(normed_two, grad_active):
        gate = dot_nn(normed_two, gate_weight)
        upward = dot_nn(normed_two, up_weight)
        active = (jax.nn.silu(gate) * upward).astype(jnp.bfloat16)
        gate_sigmoid = jax.nn.sigmoid(gate)
        grad_act_f = grad_active.astype(jnp.float32)
        grad_gate = (
            grad_act_f * upward * gate_sigmoid * (1.0 + gate * (1.0 - gate_sigmoid))
        ).astype(jnp.bfloat16)
        grad_upward = (grad_act_f * gate * gate_sigmoid).astype(jnp.bfloat16)
        return active, grad_gate, grad_upward

    active, grad_gate, grad_upward = line.run(gated, normed_two, grad_active)
    own, arrived = scatter_rows(
        line,
        lambda a, b, g, u: dot_nt(g[a:b], gate_weight) + dot_nt(u[a:b], up_weight),
        (grad_gate, grad_upward),
        LEN,
    )
    down = WeightSum(line, grad_branch, active, near)
    gate_sum = WeightSum(line, normed_two, grad_gate, near)
    up_sum = WeightSum(line, normed_two, grad_upward, near)

    def middle_grads(own, arrived):
        grad_hidden, mlp_gain_part = rms_back(hidden_rows, scale_two, mlp_gain, own + arrived)
        grad_hidden = grad_hidden + out_grad
        return grad_hidden, mlp_gain_part, grad_hidden.astype(jnp.bfloat16)

    grad_hidden, mlp_gain_part, mid_rows = line.run(middle_grads, own, arrived)
    grad_mid = gather_rows(mid_rows)
    down.step()
    gate_sum.step()
    last_own, last_arrived = scatter_rows(
        line, lambda a, b, m, w: dot_nn(m[a:b], w), (active, down_weight), LEN
    )
    up_sum.step()

    grad_mid, grad_mixed = line.run(
        lambda m, w: (m, dot_nt(m, w).astype(jnp.bfloat16)), grad_mid, output_padded
    )
    down.step()
    cut = pairs // 2
    saved = (attended, decay, log_total)
    output_sum = WeightSum(line, grad_mid, mixed[:, :width], far)
    grads_a, decay_a = line.run(
        lambda g: attention_backward(places, qkvz, g, *saved, 0, cut), grad_mixed
    )
    last_arrived = line.start(last_arrived)
    gate_sum.step()
    down.step()
    output_sum.step()
    sum_a = WeightSum(line, normed, grads_a, near)
    grads_b, decay_b = line.run(
        lambda g: attention_backward(places, qkvz, g, *saved, cut, pairs - cut), grad_mixed
    )
    sum_a.step()
    sum_b = WeightSum(line, normed, grads_b, near)
    up_sum.step()
    down.arrive()
    gate_sum.step()
    output_sum.step()
    middle = cut * 4 * LANES

    def forget_term(decay_a, decay_b):
        grad_decay = from_pairs(jnp.concatenate([decay_a, decay_b], axis=0), heads_here)
        return (running_sum(later, grad_decay) * jax.nn.sigmoid(-forget_logit)).astype(
            jnp.bfloat16
        )

    def normed_term(a, b, grads_a, grads_b, grad_forget):
        term = dot_nt(grads_a[a:b], projection[:, :middle])
        term = term + dot_nt(grads_b[a:b], projection[:, middle:])
        return term + dot_nt(grad_forget[a:b], forget_weight)

    grad_forget = line.run(forget_term, decay_a, decay_b)
    values = (grads_a, grads_b, grad_forget)
    half = LEN // 2
    if two_devices():
        sent = line.run(lambda *v: normed_term(half, LEN, *v).astype(jnp.bfloat16), *values)
        arrived = swap(sent)
    sum_b.step()
    if two_devices():
        own = line.run(lambda *v: normed_term(0, half, *v), *values)
    else:
        own, arrived = scatter_rows(line, normed_term, values, LEN)

    def small_terms(grad_forget, normed):
        bias_part = jnp.sum(grad_forget.astype(jnp.float32), axis=0)
        bias_row = lax.dynamic_update_slice_in_dim(
            jnp.zeros((normed.shape[1],), jnp.float32),
            bias_part,
            lax.axis_index("tensor") * heads_here,
            0,
        )
        return bias_row, weight_term(grad_forget, normed)

    bias_row, forget_part = line.run(small_terms, grad_forget, normed)
    sum_a.step()
    up_sum.step()

    def input_grads(own, arrived):
        input_part, attn_gain_part = rms_back(tokens_in, scale_one, attn_gain, own + arrived)
        return grad_hidden + input_part, attn_gain_part

    input_grad, attn_gain_part = line.run(input_grads, own, arrived)
    small = jnp.concatenate(
        [jnp.stack([attn_gain_part, mlp_gain_part, bias_row]), forget_part], axis=0
    )
    gains = AllSum(line, small, 3)
    sum_b.step()
    gains.step()
    output_sum.step()
    sum_a.step()
    gains.step()
    down_grad = down.result(jnp.transpose)
    gate_grad = gate_sum.result()
    layer_out = line.run(lambda a, b: hidden_rows + (a + b), last_own, last_arrived)
    sum_b.step()
    gains.step()
    output_grad = output_sum.result(jnp.transpose)
    up_grad = up_sum.result()
    top, forget_full = gains.result()
    block_rows = forget_full.shape[1] // lax.axis_size("dp")
    forget_grad = lax.dynamic_slice_in_dim(
        forget_full, lax.axis_index("dp") * block_rows, block_rows, 1
    ).T
    block = jnp.concatenate([sum_a.result(), sum_b.result()], axis=1)
    block = block.reshape(block.shape[0], pairs, 4, LANES)
    query_grad, key_grad, value_grad, outgate_grad = [
        block[:, :, part].reshape(block.shape[0], pairs * LANES)[:, :width] for part in range(4)
    ]
    attn_gain_grad, mlp_gain_grad, bias_grad = top[0] + line.token, top[1], top[2, :H]
    return (
        layer_out,
        input_grad,
        attn_gain_grad,
        query_grad,
        key_grad,
        value_grad,
        forget_grad,
        bias_grad,
        outgate_grad,
        output_grad,
        mlp_gain_grad,
        gate_grad,
        up_grad,
        down_grad,
    )


def solution(mesh):
    in_specs = (
        P(("dp", "tensor"), None),
        P("dp"),
        P(),
        P(None, "tensor"),
        P(None, "tensor"),
        P(None, "tensor"),
        P(None, "tensor"),
        P("tensor"),
        P(None, "tensor"),
        P("tensor", None),
        P(),
        P(None, "tensor"),
        P(None, "tensor"),
        P("tensor", None),
        P(("dp", "tensor"), None),
    )
    out_specs = (
        P(("dp", "tensor"), None),
        P(("dp", "tensor"), None),
        P(),
        P("dp", "tensor"),
        P("dp", "tensor"),
        P("dp", "tensor"),
        P("dp", "tensor"),
        P(),
        P("dp", "tensor"),
        P("tensor", "dp"),
        P(),
        P("dp", "tensor"),
        P("dp", "tensor"),
        P("tensor", "dp"),
    )
    return jax.shard_map(local, mesh=mesh, in_specs=in_specs, out_specs=out_specs, check_vma=False)
```

```python
import jax
import jax.numpy as jnp
from jax import lax
from jax.experimental import pallas as pl
from jax.experimental.pallas import tpu as pltpu
from jax.sharding import PartitionSpec as P

H = 24
HD = 64
LEN = 1024
LANES = 128
FAR = -1e30


epsilon = 1e-06


def dot_nn(left, right):
    return lax.dot_general(
        left, right, (((1,), (0,)), ((), ())), preferred_element_type=jnp.float32
    )


def dot_nt(left, right):
    return lax.dot_general(
        left, right, (((1,), (1,)), ((), ())), preferred_element_type=jnp.float32
    )


def dot_tn(left, right):
    return lax.dot_general(
        left, right, (((0,), (0,)), ((), ())), preferred_element_type=jnp.float32
    )


def lane_of(shape, head):
    lane = lax.broadcasted_iota(jnp.int32, shape, 1)
    return lane - (1 - head) * HD, (lane // HD) == head


def three_lanes(relative, first, column, otherwise):
    high = column.astype(jnp.bfloat16).astype(jnp.float32)
    rest = column - high
    middle = rest.astype(jnp.bfloat16).astype(jnp.float32)
    low = rest - middle
    placed = jnp.where(relative == first + 2, low, otherwise)
    placed = jnp.where(relative == first + 1, middle, placed)
    return jnp.where(relative == first, high, placed)


def lanes_at(relative, first, value, otherwise):
    return jnp.where((relative >= first) & (relative < first + 3), value, otherwise)


def quarters(ref):
    return [ref.at[:, part * LANES : (part + 1) * LANES] for part in range(4)]


def forward_kernel(slot, where_ref, qkvz_ref, d_ref, *refs):
    mixed_ref, att_ref, total_ref, qa, qu, ka = refs[-6:]
    q_ref, k_ref, v_ref, z_ref = quarters(qkvz_ref)
    length = q_ref.shape[0]
    half, quarter = length // 2, length // 4
    prefix = where_ref[0]
    here, there = slot * half, (1 - slot) * half
    is_first = where_ref[1] == here
    here_rows = pl.ds(here, half)
    for head in range(2):
        relative, own = lane_of((length, LANES), head)
        decay = jnp.broadcast_to(d_ref[0, :, head : head + 1], (length, LANES))
        minus = three_lanes(relative, 3, -decay, lanes_at(relative, 0, 1.0, 0.0))
        ka[...] = jnp.where(own, k_ref[...].astype(jnp.float32), minus).astype(jnp.bfloat16)
        relative, own = lane_of((half, LANES), head)
        decay = jnp.broadcast_to(d_ref[0, here_rows, head : head + 1], (half, LANES))
        plus = three_lanes(relative, 0, decay, lanes_at(relative, 3, 1.0, 0.0))
        scaled = q_ref[here_rows, :].astype(jnp.float32) * HD**-0.5
        qa[...] = jnp.where(own, scaled, plus).astype(jnp.bfloat16)
        qu[...] = jnp.where(own, scaled, -plus).astype(jnp.bfloat16)
        lanes = slice(head * HD, head * HD + HD)

        def finish(rows, parts, lanes=lanes, head=head):
            top = parts[0][0].max(axis=1, keepdims=True)
            for scores, _ in parts[1:]:
                top = jnp.maximum(top, scores.max(axis=1, keepdims=True))
            norm, out = 0.0, 0.0
            for scores, keys in parts:
                weight = jnp.exp(scores - top)
                norm = norm + weight.sum(axis=1, keepdims=True)
                out = out + dot_nn(weight.astype(jnp.bfloat16), v_ref[keys, :])
            att_ref[rows, lanes] = (out / norm)[:, lanes]
            total_ref[0, rows, head : head + 1] = top + jnp.log(norm)

        @pl.when(is_first)
        def _(finish=finish):
            for part in range(2):
                rows = pl.ds(part * quarter, quarter)
                i = lax.broadcasted_iota(jnp.int32, (quarter, half), 0) + part * quarter
                j = lax.broadcasted_iota(jnp.int32, (quarter, half), 1)
                both = (i < prefix) & (j < prefix)
                below = dot_nt(qa[rows, :], ka[here_rows, :])
                above = dot_nt(qu[rows, :], ka[here_rows, :])
                scores = jnp.where(j <= i, below, jnp.where(both, above, FAR))
                finish(rows, [(scores, here_rows)])

        @pl.when(jnp.logical_not(is_first))
        def _(finish=finish):
            early = pl.ds(there, half)
            for part in range(2):
                rows = pl.ds(part * quarter, quarter)
                width = (part + 1) * quarter
                late = pl.ds(here, width)
                i = lax.broadcasted_iota(jnp.int32, (quarter, width), 0) + part * quarter
                j = lax.broadcasted_iota(jnp.int32, (quarter, width), 1)
                finish(
                    rows,
                    [
                        (dot_nt(qa[rows, :], ka[early, :]), early),
                        (jnp.where(j <= i, dot_nt(qa[rows, :], ka[late, :]), FAR), late),
                    ],
                )

    outgate = jax.nn.sigmoid(z_ref[here_rows, :].astype(jnp.float32))
    mixed_ref[...] = (outgate * att_ref[...]).astype(jnp.bfloat16)


def backward_kernel(
    where_ref,
    qkvz_ref,
    gm_ref,
    att_ref,
    d_ref,
    total_ref,
    grads_ref,
    gd_ref,
    qa,
    qu,
    ka,
    va,
    ga,
    acc_q,
    acc_k,
    acc_v,
):
    q_ref, k_ref, v_ref, z_ref = quarters(qkvz_ref)
    dq_ref, dk_ref, dv_ref, dz_ref = quarters(grads_ref)
    length = q_ref.shape[0]
    half, quarter = length // 2, length // 4
    prefix, first, second = where_ref[0], where_ref[1], where_ref[2]
    first = pl.multiple_of(first, half)
    second = pl.multiple_of(second, half)
    outgate = jax.nn.sigmoid(z_ref[...].astype(jnp.float32))
    grad_mixed = gm_ref[...].astype(jnp.float32)
    attended = att_ref[...]
    grad_att = (grad_mixed * outgate).astype(jnp.bfloat16).astype(jnp.float32)
    dz_ref[...] = (grad_mixed * attended * outgate * (1.0 - outgate)).astype(jnp.bfloat16)
    product = grad_att * attended
    for head in range(2):
        relative, own = lane_of((length, LANES), head)
        delta = jnp.sum(jnp.where(own, product, 0.0), axis=1, keepdims=True)
        delta = jnp.broadcast_to(delta, (length, LANES))
        decay = jnp.broadcast_to(d_ref[0, :, head : head + 1], (length, LANES))
        total = jnp.broadcast_to(total_ref[0, :, head : head + 1], (length, LANES))
        ones = lanes_at(relative, 3, 1.0, 0.0)
        ones_front = lanes_at(relative, 0, 1.0, 0.0)
        scaled = q_ref[...].astype(jnp.float32) * HD**-0.5
        qa[...] = jnp.where(own, scaled, three_lanes(relative, 0, decay - total, ones)).astype(
            jnp.bfloat16
        )
        qu[...] = jnp.where(own, scaled, three_lanes(relative, 0, -decay - total, -ones)).astype(
            jnp.bfloat16
        )
        ka[...] = jnp.where(
            own, k_ref[...].astype(jnp.float32), three_lanes(relative, 3, -decay, ones_front)
        ).astype(jnp.bfloat16)
        va[...] = jnp.where(own, v_ref[...].astype(jnp.float32), ones_front).astype(jnp.bfloat16)
        ga[...] = jnp.where(own, grad_att, three_lanes(relative, 0, -delta, 0.0)).astype(
            jnp.bfloat16
        )
        lanes = slice(head * HD, head * HD + HD)
        free = (1 - head) * HD

        def unit(keys, queries, shape, key_start, query_start, prefixed, masked, fresh_k, fresh_q,
                 head=head):
            score = dot_nt(ka[keys, :], qa[queries, :])
            if prefixed or masked:
                j = lax.broadcasted_iota(jnp.int32, shape, 0) + key_start
                i = lax.broadcasted_iota(jnp.int32, shape, 1) + query_start
                causal = j <= i
                other = FAR
                if prefixed:
                    above = dot_nt(ka[keys, :], qu[queries, :])
                    other = jnp.where((i < prefix) & (j < prefix), above, FAR)
                score = jnp.where(causal, score, other)
            probs = jnp.exp(score)
            grad = (probs * dot_nt(va[keys, :], ga[queries, :])).astype(jnp.bfloat16)
            part_v = dot_nn(probs.astype(jnp.bfloat16), ga[queries, :])
            part_k = dot_nn(grad, qa[queries, :])
            part_q = dot_tn(grad, ka[keys, :])
            if prefixed:
                turned = jnp.where(causal, 0.0, -2.0 * grad.astype(jnp.float32)).astype(
                    jnp.bfloat16
                )
                back_k, _ = lane_of((shape[1], LANES), head)
                back_q, _ = lane_of((shape[0], LANES), head)
                part_k = part_k + dot_nn(turned, jnp.where(back_k == 3, 1.0, 0.0).astype(jnp.bfloat16))
                part_q = part_q + dot_tn(turned, jnp.where(back_q == 0, 1.0, 0.0).astype(jnp.bfloat16))
            if fresh_k:
                acc_k[keys, :] = part_k
                acc_v[keys, :] = part_v
            else:
                acc_k[keys, :] += part_k
                acc_v[keys, :] += part_v
            if fresh_q:
                acc_q[queries, :] = part_q
            else:
                acc_q[queries, :] += part_q

        early = pl.ds(first, half)
        for part in range(2):
            queries = pl.ds(first + part * quarter, quarter)
            unit(early, queries, (half, quarter), 0, part * quarter, True, False, part == 0, True)
        for part in range(2):
            queries = pl.ds(second + part * quarter, quarter)
            unit(early, queries, (half, quarter), 0, 0, False, False, False, True)
        unit(pl.ds(second, half), pl.ds(second + quarter, quarter), (half, quarter), 0, quarter,
             False, True, True, False)
        unit(pl.ds(second, quarter), pl.ds(second, quarter), (quarter, quarter), 0, 0,
             False, True, False, False)
        dq_ref[:, lanes] = (acc_q[:, lanes] * HD**-0.5).astype(jnp.bfloat16)
        dk_ref[:, lanes] = acc_k[:, lanes].astype(jnp.bfloat16)
        dv_ref[:, lanes] = acc_v[:, lanes].astype(jnp.bfloat16)
        gd_ref[0, :, head : head + 1] = acc_q[:, free : free + 1] - acc_k[:, free + 3 : free + 4]


def wide(length, columns, offset=0):
    return pl.BlockSpec((length, columns), lambda pair, where: (0, pair + offset))


def narrow(length, offset=0):
    return pl.BlockSpec((1, length, 2), lambda pair, where: (pair + offset, 0, 0))


def attention_forward(places, qkvz, decay, slot, before=None):
    length = qkvz.shape[0]
    half = length // 2
    pairs = decay.shape[0]
    rows = pl.BlockSpec((half, LANES), lambda pair, where: (slot, pair))
    column = pl.BlockSpec((1, half, 2), lambda pair, where: (pair, slot, 0))
    held = () if before is None else tuple(before)
    return pl.pallas_call(
        lambda *refs: forward_kernel(slot, *refs),
        grid_spec=pltpu.PrefetchScalarGridSpec(
            num_scalar_prefetch=1,
            grid=(pairs,),
            in_specs=[wide(length, 4 * LANES), narrow(length)]
            + [pl.BlockSpec(memory_space=pl.ANY)] * len(held),
            out_specs=[rows, rows, column],
            scratch_shapes=[pltpu.VMEM((half, LANES), jnp.bfloat16)] * 2
            + [pltpu.VMEM((length, LANES), jnp.bfloat16)],
        ),
        out_shape=[
            jax.ShapeDtypeStruct((length, pairs * LANES), jnp.bfloat16),
            jax.ShapeDtypeStruct((length, pairs * LANES), jnp.float32),
            jax.ShapeDtypeStruct((pairs, length, 2), jnp.float32),
        ],
        input_output_aliases={3 + k: k for k in range(len(held))},
        compiler_params=pltpu.CompilerParams(vmem_limit_bytes=56 << 20),
        cost_estimate=pl.CostEstimate(
            flops=1_000_000, bytes_accessed=1_000_000, transcendentals=0
        ),
        name="attention_forward",
    )(places, qkvz, decay, *held)


def attention_backward(places, qkvz, grad_mixed, attended, decay, log_total, start, count):
    length = qkvz.shape[0]
    return pl.pallas_call(
        backward_kernel,
        grid_spec=pltpu.PrefetchScalarGridSpec(
            num_scalar_prefetch=1,
            grid=(count,),
            in_specs=[wide(length, 4 * LANES, start)]
            + [wide(length, LANES, start)] * 2
            + [narrow(length, start)] * 2,
            out_specs=[wide(length, 4 * LANES), narrow(length)],
            scratch_shapes=[pltpu.VMEM((length, LANES), jnp.bfloat16)] * 5
            + [pltpu.VMEM((length, LANES), jnp.float32)] * 3,
        ),
        out_shape=[
            jax.ShapeDtypeStruct((length, count * 4 * LANES), jnp.bfloat16),
            jax.ShapeDtypeStruct((count, length, 2), jnp.float32),
        ],
        compiler_params=pltpu.CompilerParams(vmem_limit_bytes=56 << 20),
        cost_estimate=pl.CostEstimate(
            flops=7_000_000_000, bytes_accessed=10_000_000, transcendentals=0
        ),
        name="attention_backward",
    )(places, qkvz, grad_mixed, attended, decay, log_total)


def weight_term(left, right):
    return lax.dot_general(
        left, right, (((0,), (0,)), ((), ())), preferred_element_type=jnp.float32
    )


def rms_rows(rows, gain):
    inverse = lax.rsqrt(jnp.mean(rows * rows, axis=-1, keepdims=True) + epsilon)
    return (inverse, rows * inverse * gain)


def rms_back(rows, inverse, gain, grad):
    scaled = grad * gain
    gain_term = jnp.sum(grad * rows * inverse, axis=0)
    row_term = inverse * scaled - rows * inverse**3 * jnp.mean(
        scaled * rows, axis=-1, keepdims=True
    )
    return (row_term, gain_term)


def tie(*values):
    return lax.optimization_barrier(values)


def swap(rows):
    return lax.ppermute(rows, "tensor", [(0, 1), (1, 0)])


def two_devices():
    return lax.axis_size("tensor") == 2


def gather_rows(rows, other=None):
    if not two_devices():
        return lax.all_gather(rows, "tensor", axis=0, tiled=True)
    return jnp.concatenate([rows, swap(rows) if other is None else other], axis=0)


def half_starts(length):
    if not two_devices():
        return jnp.array(0, jnp.int32), jnp.array(length // 2, jnp.int32)
    first = lax.axis_index("tensor") * (length // 2)
    return first, length // 2 - first


class Line:
    def __init__(self):
        self.token = jnp.zeros((), jnp.float32)

    def start(self, values):
        self.token, values = tie(self.token, values)
        return values

    def run(self, step, *values):
        return self.start(step(*self.start(values)))


def scatter_rows(line, product, values, length):
    if not two_devices():
        term = line.run(lambda *v: product(0, length, *v).astype(jnp.bfloat16), *values)
        return lax.psum_scatter(term, "tensor", scatter_dimension=0, tiled=True), jnp.zeros(
            (), jnp.bfloat16
        )
    terms = line.run(lambda *v: product(0, length, *v), *values)
    sent = line.run(lambda t: t[length // 2 :].astype(jnp.bfloat16), terms)
    return terms[: length // 2], swap(sent)


def halves_kernel(mine_ref, left_ref, right_ref, kept_ref, sent_ref, total):
    total[...] = dot_tn(left_ref[...], right_ref[...])
    count, rows, _ = kept_ref.shape
    mine = mine_ref[0]
    for pair in range(count):
        for ref, place in ((kept_ref, mine), (sent_ref, 1 - mine)):
            start = pl.multiple_of((2 * pair + place) * rows, 8)
            ref[pair] = total[pl.ds(start, rows), :].astype(ref.dtype)


def weight_halves(left, right, size):
    length, rows = left.shape
    columns = right.shape[1]
    step = 384
    block = rows // size
    assert rows % step == 0 and step % (2 * block) == 0
    count = step // (2 * block)
    mine = (lax.axis_index("dp") % 2).reshape(1)
    half = pl.BlockSpec((count, block, columns), lambda i, mine: (i, 0, 0))
    return pl.pallas_call(
        halves_kernel,
        grid_spec=pltpu.PrefetchScalarGridSpec(
            num_scalar_prefetch=1,
            grid=(rows // step,),
            in_specs=[
                pl.BlockSpec((length, step), lambda i, mine: (0, i)),
                pl.BlockSpec((length, columns), lambda i, mine: (0, 0)),
            ],
            out_specs=[half, half],
            scratch_shapes=[pltpu.VMEM((step, columns), jnp.float32)],
        ),
        out_shape=[jax.ShapeDtypeStruct((size // 2, block, columns), jnp.bfloat16)] * 2,
        compiler_params=pltpu.CompilerParams(vmem_limit_bytes=40 << 20),
        cost_estimate=pl.CostEstimate(flops=1_000_000, bytes_accessed=1_000_000, transcendentals=0),
        name="weight_halves",
    )(mine, left, right)


def halve_kernel(mine_ref, kept_a, sent_a, kept_b, sent_b, kept_ref, sent_ref):
    kept = kept_a[...].astype(jnp.float32) + kept_b[...].astype(jnp.float32)
    sent = sent_a[...].astype(jnp.float32) + sent_b[...].astype(jnp.float32)
    kept_ref[...] = kept.astype(kept_ref.dtype)
    sent_ref[...] = sent.astype(sent_ref.dtype)


def halve(one, two, axis, mine):
    lead, (rows, columns) = one.shape[:-2], one.shape[-2:]
    before = 2**axis
    after = 2 ** (len(lead) - axis - 1)
    cut = (before, 2, after, rows, columns)
    block = (1, pl.squeezed, 1, rows, columns)
    kept = pl.BlockSpec(block, lambda p, q, mine: (p, mine[0], q, 0, 0))
    sent = pl.BlockSpec(block, lambda p, q, mine: (p, 1 - mine[0], q, 0, 0))
    out = pl.BlockSpec((1, 1, rows, columns), lambda p, q, mine: (p, q, 0, 0))
    one, two = one.reshape(cut), two.reshape(cut)
    parts = pl.pallas_call(
        halve_kernel,
        grid_spec=pltpu.PrefetchScalarGridSpec(
            num_scalar_prefetch=1,
            grid=(before, after),
            in_specs=[kept, sent, kept, sent],
            out_specs=[out, out],
        ),
        out_shape=[jax.ShapeDtypeStruct((before, after, rows, columns), one.dtype)] * 2,
        compiler_params=pltpu.CompilerParams(vmem_limit_bytes=40 << 20),
        cost_estimate=pl.CostEstimate(flops=1_000_000, bytes_accessed=1_000_000, transcendentals=0),
        name="halve",
    )(mine.reshape(1), one, one, two, two)
    shape = lead[:axis] + lead[axis + 1 :] + (rows, columns)
    return [part.reshape(shape) for part in parts]


class WeightSum:
    def __init__(self, line, left, right, masks):
        self.line = line
        self.size = lax.axis_size("dp")
        self.bits = self.size.bit_length() - 1
        kept, sent = line.run(lambda *v: weight_halves(*v, self.size), left, right)
        shape = (2,) * (self.bits - 1) + kept.shape[1:]
        assert masks[0] == 1
        self.masks = list(masks[1:])
        self.left = list(range(self.bits - 1, 0, -1))
        self.terms = [kept.reshape(shape), self.exchange(sent.reshape(shape), 1)]

    def exchange(self, sent, mask):
        return lax.ppermute(sent, "dp", [(i, i ^ mask) for i in range(self.size)])

    def arrive(self):
        self.terms[-1] = self.line.start(self.terms[-1])

    def step(self):
        if not self.masks:
            return
        mask = self.masks.pop(0)
        axis = self.left.index(mask.bit_length() - 1)
        self.left.remove(mask.bit_length() - 1)
        mine = (lax.axis_index("dp") // mask) % 2
        kept, sent = self.line.run(lambda *t: halve(*t, axis, mine), *self.terms)
        self.terms = [kept, self.exchange(sent, mask)]

    def result(self, finish=lambda total: total):
        while self.masks:
            self.step()
        return self.line.run(
            lambda *terms: finish(sum(term.astype(jnp.float32) for term in terms)), *self.terms
        )


class AllSum:
    def __init__(self, line, value, rows):
        self.line, self.value, self.rows, self.mask = line, value, rows, 1
        self.arrived = jnp.zeros((), value.dtype)
        self.step()

    def step(self):
        size = lax.axis_size("dp")
        if self.mask < size:
            mask = self.mask
            self.value = self.line.run(lambda a, b: a + b, self.value, self.arrived)
            self.arrived = lax.ppermute(self.value, "dp", [(i, i ^ mask) for i in range(size)])
            self.mask *= 2

    def result(self):
        while self.mask < lax.axis_size("dp"):
            self.step()
        value = self.line.run(lambda a, b: a + b, self.value, self.arrived)
        top = value[: self.rows]
        if not two_devices():
            return lax.psum(top, "tensor"), value[self.rows :]
        return self.line.run(lambda a, b: a + b, top, swap(top)), value[self.rows :]


def pair_columns(weights, pairs):
    width = pairs * LANES
    padded = [jnp.pad(w, ((0, 0), (0, width - w.shape[1]))) for w in weights]
    parts = [w[:, p * LANES : (p + 1) * LANES] for p in range(pairs) for w in padded]
    return jnp.concatenate(parts, axis=1)


def running_sum(order, values):
    high = lax.reduce_precision(values, 8, 7)
    middle = lax.reduce_precision(values - high, 8, 7)
    terms = jnp.concatenate([high, middle, values - high - middle], axis=1).astype(jnp.bfloat16)
    sums = dot_nn(order, terms)
    return sum(jnp.split(sums, 3, axis=1))


def by_pairs(columns):
    length, heads = columns.shape
    columns = jnp.pad(columns, ((0, 0), (0, heads % 2)))
    return columns.reshape(length, -1, 2).transpose(1, 0, 2)


def from_pairs(pairs, heads):
    return pairs.transpose(1, 0, 2).reshape(pairs.shape[1], -1)[:, :heads]


def local(
    tokens_in,
    prefix_len,
    attn_gain,
    query_weight,
    key_weight,
    value_weight,
    forget_weight,
    forget_bias,
    outgate_weight,
    output_weight,
    mlp_gain,
    gate_weight,
    up_weight,
    down_weight,
    out_grad,
):
    heads_here = forget_weight.shape[1]
    assert prefix_len.shape[0] == 1
    pairs = (heads_here + 1) // 2
    width = heads_here * HD
    first, second = half_starts(LEN)
    places = jnp.stack([prefix_len[0], first, second])
    index = jnp.arange(LEN, dtype=jnp.int32)
    position = (index + first) % LEN
    earlier = (position[None, :] <= position[:, None]).astype(jnp.bfloat16)
    later = (position[None, :] >= position[:, None]).astype(jnp.bfloat16)
    bits = lax.axis_size("dp").bit_length() - 1
    near = [1 << bit for bit in range(bits)]
    far = near[:1] + near[2:] + near[1:2]

    scale_one, normed_rows = rms_rows(tokens_in, attn_gain)
    normed = gather_rows(normed_rows.astype(jnp.bfloat16))
    projection = pair_columns((query_weight, key_weight, value_weight, outgate_weight), pairs)
    output_padded = jnp.pad(output_weight, ((0, pairs * LANES - width), (0, 0)))
    normed, branch_rows = tie(normed, out_grad.astype(jnp.bfloat16))
    grad_branch = gather_rows(branch_rows)
    qkvz = dot_nn(normed, projection).astype(jnp.bfloat16)
    forget_logit = dot_nn(normed, forget_weight) + forget_bias
    decay = by_pairs(running_sum(earlier, jax.nn.log_sigmoid(forget_logit)))
    line = Line()
    saved = line.run(lambda d, q: attention_forward(places, q, d, 1), decay, qkvz)
    grad_branch = line.start(grad_branch)
    half = LEN // 2
    if two_devices():
        sent = line.run(
            lambda m: dot_nn(m[half:], output_padded).astype(jnp.bfloat16), saved[0]
        )
        arrived = swap(sent)
    saved = line.run(lambda d, q, *b: attention_forward(places, q, d, 0, b), decay, qkvz, *saved)
    mixed, attended, log_total = saved
    if two_devices():
        own = line.run(lambda m: dot_nn(m[:half], output_padded), mixed)
    else:
        own, arrived = scatter_rows(
            line, lambda a, b, m, w: dot_nn(m[a:b], w), (mixed, output_padded), LEN
        )
    hidden_rows = tokens_in + line.run(lambda a, b: a + b, own, arrived)

    scale_two, normed_two_rows = rms_rows(hidden_rows, mlp_gain)
    normed_two = gather_rows(line.start(normed_two_rows.astype(jnp.bfloat16)))
    grad_active = line.run(
        lambda g, w: dot_nt(g, w).astype(jnp.bfloat16), grad_branch, down_weight
    )

    def gated(normed_two, grad_active):
        gate = dot_nn(normed_two, gate_weight)
        upward = dot_nn(normed_two, up_weight)
        active = (jax.nn.silu(gate) * upward).astype(jnp.bfloat16)
        gate_sigmoid = jax.nn.sigmoid(gate)
        grad_act_f = grad_active.astype(jnp.float32)
        grad_gate = (
            grad_act_f * upward * gate_sigmoid * (1.0 + gate * (1.0 - gate_sigmoid))
        ).astype(jnp.bfloat16)
        grad_upward = (grad_act_f * gate * gate_sigmoid).astype(jnp.bfloat16)
        return active, grad_gate, grad_upward

    active, grad_gate, grad_upward = line.run(gated, normed_two, grad_active)
    own, arrived = scatter_rows(
        line,
        lambda a, b, g, u: dot_nt(g[a:b], gate_weight) + dot_nt(u[a:b], up_weight),
        (grad_gate, grad_upward),
        LEN,
    )
    down = WeightSum(line, grad_branch, active, near)
    gate_sum = WeightSum(line, normed_two, grad_gate, near)
    up_sum = WeightSum(line, normed_two, grad_upward, near)

    def middle_grads(own, arrived):
        grad_hidden, mlp_gain_part = rms_back(hidden_rows, scale_two, mlp_gain, own + arrived)
        grad_hidden = grad_hidden + out_grad
        return grad_hidden, mlp_gain_part, grad_hidden.astype(jnp.bfloat16)

    grad_hidden, mlp_gain_part, mid_rows = line.run(middle_grads, own, arrived)
    grad_mid = gather_rows(mid_rows)
    down.step()
    gate_sum.step()
    last_own, last_arrived = scatter_rows(
        line, lambda a, b, m, w: dot_nn(m[a:b], w), (active, down_weight), LEN
    )
    up_sum.step()

    grad_mid, grad_mixed = line.run(
        lambda m, w: (m, dot_nt(m, w).astype(jnp.bfloat16)), grad_mid, output_padded
    )
    down.step()
    cut = pairs // 2
    saved = (attended, decay, log_total)
    output_sum = WeightSum(line, grad_mid, mixed[:, :width], far)
    grads_a, decay_a = line.run(
        lambda g: attention_backward(places, qkvz, g, *saved, 0, cut), grad_mixed
    )
    last_arrived = line.start(last_arrived)
    gate_sum.step()
    down.step()
    output_sum.step()
    sum_a = WeightSum(line, normed, grads_a, near)
    grads_b, decay_b = line.run(
        lambda g: attention_backward(places, qkvz, g, *saved, cut, pairs - cut), grad_mixed
    )
    sum_a.step()
    sum_b = WeightSum(line, normed, grads_b, near)
    up_sum.step()
    down.arrive()
    gate_sum.step()
    output_sum.step()
    middle = cut * 4 * LANES

    def forget_term(decay_a, decay_b):
        grad_decay = from_pairs(jnp.concatenate([decay_a, decay_b], axis=0), heads_here)
        return (running_sum(later, grad_decay) * jax.nn.sigmoid(-forget_logit)).astype(
            jnp.bfloat16
        )

    def normed_term(a, b, grads_a, grads_b, grad_forget):
        term = dot_nt(grads_a[a:b], projection[:, :middle])
        term = term + dot_nt(grads_b[a:b], projection[:, middle:])
        return term + dot_nt(grad_forget[a:b], forget_weight)

    grad_forget = line.run(forget_term, decay_a, decay_b)
    sum_a.step()
    values = (grads_a, grads_b, grad_forget)
    if two_devices():
        sent = line.run(lambda *v: normed_term(half, LEN, *v).astype(jnp.bfloat16), *values)
        arrived = swap(sent)
    up_sum.arrive()
    gate_sum.arrive()
    sum_b.step()
    if two_devices():
        own = line.run(lambda *v: normed_term(0, half, *v), *values)
    else:
        own, arrived = scatter_rows(line, normed_term, values, LEN)

    up_sum.step()
    output_sum.arrive()

    def small_terms(grad_forget, normed):
        bias_part = jnp.sum(grad_forget.astype(jnp.float32), axis=0)
        bias_row = lax.dynamic_update_slice_in_dim(
            jnp.zeros((normed.shape[1],), jnp.float32),
            bias_part,
            lax.axis_index("tensor") * heads_here,
            0,
        )
        return bias_row, weight_term(grad_forget, normed)

    bias_row, forget_part = line.run(small_terms, grad_forget, normed)
    sum_a.step()

    def input_grads(own, arrived):
        input_part, attn_gain_part = rms_back(tokens_in, scale_one, attn_gain, own + arrived)
        return grad_hidden + input_part, attn_gain_part

    sum_b.arrive()
    input_grad, attn_gain_part = line.run(input_grads, own, arrived)
    small = jnp.concatenate(
        [jnp.stack([attn_gain_part, mlp_gain_part, bias_row]), forget_part], axis=0
    )
    gains = AllSum(line, small, 3)
    sum_b.step()
    gains.step()
    up_sum.arrive()
    output_sum.step()
    sum_a.arrive()
    down_grad = down.result(jnp.transpose)
    gate_grad = gate_sum.result()
    layer_out = line.run(lambda a, b: hidden_rows + (a + b), last_own, last_arrived)
    gains.step()
    sum_b.step()
    gains.step()
    output_grad = output_sum.result(jnp.transpose)
    up_grad = up_sum.result()
    top, forget_full = gains.result()
    block_rows = forget_full.shape[1] // lax.axis_size("dp")
    forget_grad = lax.dynamic_slice_in_dim(
        forget_full, lax.axis_index("dp") * block_rows, block_rows, 1
    ).T
    block = jnp.concatenate([sum_a.result(), sum_b.result()], axis=1)
    block = block.reshape(block.shape[0], pairs, 4, LANES)
    query_grad, key_grad, value_grad, outgate_grad = [
        block[:, :, part].reshape(block.shape[0], pairs * LANES)[:, :width] for part in range(4)
    ]
    attn_gain_grad, mlp_gain_grad, bias_grad = top[0] + line.token, top[1], top[2, :H]
    return (
        layer_out,
        input_grad,
        attn_gain_grad,
        query_grad,
        key_grad,
        value_grad,
        forget_grad,
        bias_grad,
        outgate_grad,
        output_grad,
        mlp_gain_grad,
        gate_grad,
        up_grad,
        down_grad,
    )


def solution(mesh):
    in_specs = (
        P(("dp", "tensor"), None),
        P("dp"),
        P(),
        P(None, "tensor"),
        P(None, "tensor"),
        P(None, "tensor"),
        P(None, "tensor"),
        P("tensor"),
        P(None, "tensor"),
        P("tensor", None),
        P(),
        P(None, "tensor"),
        P(None, "tensor"),
        P("tensor", None),
        P(("dp", "tensor"), None),
    )
    out_specs = (
        P(("dp", "tensor"), None),
        P(("dp", "tensor"), None),
        P(),
        P("dp", "tensor"),
        P("dp", "tensor"),
        P("dp", "tensor"),
        P("dp", "tensor"),
        P(),
        P("dp", "tensor"),
        P("tensor", "dp"),
        P(),
        P("dp", "tensor"),
        P("dp", "tensor"),
        P("tensor", "dp"),
    )
    return jax.shard_map(local, mesh=mesh, in_specs=in_specs, out_specs=out_specs, check_vma=False)
```

```python
import jax
import jax.numpy as jnp
from jax import lax
from jax.experimental import pallas as pl
from jax.experimental.pallas import tpu as pltpu
from jax.sharding import PartitionSpec as P

H = 24
HD = 64
LEN = 1024
LANES = 128
FAR = -1e30


epsilon = 1e-06


def dot_nn(left, right):
    return lax.dot_general(
        left, right, (((1,), (0,)), ((), ())), preferred_element_type=jnp.float32
    )


def dot_nt(left, right):
    return lax.dot_general(
        left, right, (((1,), (1,)), ((), ())), preferred_element_type=jnp.float32
    )


def dot_tn(left, right):
    return lax.dot_general(
        left, right, (((0,), (0,)), ((), ())), preferred_element_type=jnp.float32
    )


def lane_of(shape, head):
    lane = lax.broadcasted_iota(jnp.int32, shape, 1)
    return lane - (1 - head) * HD, (lane // HD) == head


def three_lanes(relative, first, column, otherwise):
    high = column.astype(jnp.bfloat16).astype(jnp.float32)
    rest = column - high
    middle = rest.astype(jnp.bfloat16).astype(jnp.float32)
    low = rest - middle
    placed = jnp.where(relative == first + 2, low, otherwise)
    placed = jnp.where(relative == first + 1, middle, placed)
    return jnp.where(relative == first, high, placed)


def lanes_at(relative, first, value, otherwise):
    return jnp.where((relative >= first) & (relative < first + 3), value, otherwise)


def quarters(ref):
    return [ref.at[:, part * LANES : (part + 1) * LANES] for part in range(4)]


def forward_kernel(slot, where_ref, qkvz_ref, d_ref, *refs):
    mixed_ref, att_ref, total_ref, qa, qu, ka = refs[-6:]
    q_ref, k_ref, v_ref, z_ref = quarters(qkvz_ref)
    length = q_ref.shape[0]
    half, quarter = length // 2, length // 4
    prefix = where_ref[0]
    here, there = slot * half, (1 - slot) * half
    is_first = where_ref[1] == here
    here_rows = pl.ds(here, half)
    for head in range(2):
        relative, own = lane_of((length, LANES), head)
        decay = jnp.broadcast_to(d_ref[0, :, head : head + 1], (length, LANES))
        minus = three_lanes(relative, 3, -decay, lanes_at(relative, 0, 1.0, 0.0))
        ka[...] = jnp.where(own, k_ref[...].astype(jnp.float32), minus).astype(jnp.bfloat16)
        relative, own = lane_of((half, LANES), head)
        decay = jnp.broadcast_to(d_ref[0, here_rows, head : head + 1], (half, LANES))
        plus = three_lanes(relative, 0, decay, lanes_at(relative, 3, 1.0, 0.0))
        scaled = q_ref[here_rows, :].astype(jnp.float32) * HD**-0.5
        qa[...] = jnp.where(own, scaled, plus).astype(jnp.bfloat16)
        qu[...] = jnp.where(own, scaled, -plus).astype(jnp.bfloat16)
        lanes = slice(head * HD, head * HD + HD)

        def finish(rows, parts, lanes=lanes, head=head):
            top = parts[0][0].max(axis=1, keepdims=True)
            for scores, _ in parts[1:]:
                top = jnp.maximum(top, scores.max(axis=1, keepdims=True))
            norm, out = 0.0, 0.0
            for scores, keys in parts:
                weight = jnp.exp(scores - top)
                norm = norm + weight.sum(axis=1, keepdims=True)
                out = out + dot_nn(weight.astype(jnp.bfloat16), v_ref[keys, :])
            att_ref[rows, lanes] = (out / norm)[:, lanes]
            total_ref[0, rows, head : head + 1] = top + jnp.log(norm)

        @pl.when(is_first)
        def _(finish=finish):
            for part in range(2):
                rows = pl.ds(part * quarter, quarter)
                i = lax.broadcasted_iota(jnp.int32, (quarter, half), 0) + part * quarter
                j = lax.broadcasted_iota(jnp.int32, (quarter, half), 1)
                both = (i < prefix) & (j < prefix)
                below = dot_nt(qa[rows, :], ka[here_rows, :])
                above = dot_nt(qu[rows, :], ka[here_rows, :])
                scores = jnp.where(j <= i, below, jnp.where(both, above, FAR))
                finish(rows, [(scores, here_rows)])

        @pl.when(jnp.logical_not(is_first))
        def _(finish=finish):
            early = pl.ds(there, half)
            for part in range(2):
                rows = pl.ds(part * quarter, quarter)
                width = (part + 1) * quarter
                late = pl.ds(here, width)
                i = lax.broadcasted_iota(jnp.int32, (quarter, width), 0) + part * quarter
                j = lax.broadcasted_iota(jnp.int32, (quarter, width), 1)
                finish(
                    rows,
                    [
                        (dot_nt(qa[rows, :], ka[early, :]), early),
                        (jnp.where(j <= i, dot_nt(qa[rows, :], ka[late, :]), FAR), late),
                    ],
                )

    outgate = jax.nn.sigmoid(z_ref[here_rows, :].astype(jnp.float32))
    mixed_ref[...] = (outgate * att_ref[...]).astype(jnp.bfloat16)


def backward_kernel(
    where_ref,
    qkvz_ref,
    gm_ref,
    att_ref,
    d_ref,
    total_ref,
    grads_ref,
    gd_ref,
    qa,
    qu,
    ka,
    va,
    ga,
    acc_q,
    acc_k,
    acc_v,
):
    q_ref, k_ref, v_ref, z_ref = quarters(qkvz_ref)
    dq_ref, dk_ref, dv_ref, dz_ref = quarters(grads_ref)
    length = q_ref.shape[0]
    half, quarter = length // 2, length // 4
    prefix, first, second = where_ref[0], where_ref[1], where_ref[2]
    first = pl.multiple_of(first, half)
    second = pl.multiple_of(second, half)
    outgate = jax.nn.sigmoid(z_ref[...].astype(jnp.float32))
    grad_mixed = gm_ref[...].astype(jnp.float32)
    attended = att_ref[...]
    grad_att = (grad_mixed * outgate).astype(jnp.bfloat16).astype(jnp.float32)
    dz_ref[...] = (grad_mixed * attended * outgate * (1.0 - outgate)).astype(jnp.bfloat16)
    product = grad_att * attended
    for head in range(2):
        relative, own = lane_of((length, LANES), head)
        delta = jnp.sum(jnp.where(own, product, 0.0), axis=1, keepdims=True)
        delta = jnp.broadcast_to(delta, (length, LANES))
        decay = jnp.broadcast_to(d_ref[0, :, head : head + 1], (length, LANES))
        total = jnp.broadcast_to(total_ref[0, :, head : head + 1], (length, LANES))
        ones = lanes_at(relative, 3, 1.0, 0.0)
        ones_front = lanes_at(relative, 0, 1.0, 0.0)
        scaled = q_ref[...].astype(jnp.float32) * HD**-0.5
        qa[...] = jnp.where(own, scaled, three_lanes(relative, 0, decay - total, ones)).astype(
            jnp.bfloat16
        )
        qu[...] = jnp.where(own, scaled, three_lanes(relative, 0, -decay - total, -ones)).astype(
            jnp.bfloat16
        )
        ka[...] = jnp.where(
            own, k_ref[...].astype(jnp.float32), three_lanes(relative, 3, -decay, ones_front)
        ).astype(jnp.bfloat16)
        va[...] = jnp.where(own, v_ref[...].astype(jnp.float32), ones_front).astype(jnp.bfloat16)
        ga[...] = jnp.where(own, grad_att, three_lanes(relative, 0, -delta, 0.0)).astype(
            jnp.bfloat16
        )
        lanes = slice(head * HD, head * HD + HD)
        free = (1 - head) * HD

        def unit(keys, queries, shape, key_start, query_start, prefixed, masked, fresh_k, fresh_q,
                 head=head):
            score = dot_nt(ka[keys, :], qa[queries, :])
            if prefixed or masked:
                j = lax.broadcasted_iota(jnp.int32, shape, 0) + key_start
                i = lax.broadcasted_iota(jnp.int32, shape, 1) + query_start
                causal = j <= i
                other = FAR
                if prefixed:
                    above = dot_nt(ka[keys, :], qu[queries, :])
                    other = jnp.where((i < prefix) & (j < prefix), above, FAR)
                score = jnp.where(causal, score, other)
            probs = jnp.exp(score)
            grad = (probs * dot_nt(va[keys, :], ga[queries, :])).astype(jnp.bfloat16)
            part_v = dot_nn(probs.astype(jnp.bfloat16), ga[queries, :])
            part_k = dot_nn(grad, qa[queries, :])
            part_q = dot_tn(grad, ka[keys, :])
            if prefixed:
                turned = jnp.where(causal, 0.0, -2.0 * grad.astype(jnp.float32)).astype(
                    jnp.bfloat16
                )
                back_k, _ = lane_of((shape[1], LANES), head)
                back_q, _ = lane_of((shape[0], LANES), head)
                part_k = part_k + dot_nn(turned, jnp.where(back_k == 3, 1.0, 0.0).astype(jnp.bfloat16))
                part_q = part_q + dot_tn(turned, jnp.where(back_q == 0, 1.0, 0.0).astype(jnp.bfloat16))
            if fresh_k:
                acc_k[keys, :] = part_k
                acc_v[keys, :] = part_v
            else:
                acc_k[keys, :] += part_k
                acc_v[keys, :] += part_v
            if fresh_q:
                acc_q[queries, :] = part_q
            else:
                acc_q[queries, :] += part_q

        early = pl.ds(first, half)
        for part in range(2):
            queries = pl.ds(first + part * quarter, quarter)
            unit(early, queries, (half, quarter), 0, part * quarter, True, False, part == 0, True)
        for part in range(2):
            queries = pl.ds(second + part * quarter, quarter)
            unit(early, queries, (half, quarter), 0, 0, False, False, False, True)
        unit(pl.ds(second, half), pl.ds(second + quarter, quarter), (half, quarter), 0, quarter,
             False, True, True, False)
        unit(pl.ds(second, quarter), pl.ds(second, quarter), (quarter, quarter), 0, 0,
             False, True, False, False)
        dq_ref[:, lanes] = (acc_q[:, lanes] * HD**-0.5).astype(jnp.bfloat16)
        dk_ref[:, lanes] = acc_k[:, lanes].astype(jnp.bfloat16)
        dv_ref[:, lanes] = acc_v[:, lanes].astype(jnp.bfloat16)
        gd_ref[0, :, head : head + 1] = acc_q[:, free : free + 1] - acc_k[:, free + 3 : free + 4]


def wide(length, columns, offset=0):
    return pl.BlockSpec((length, columns), lambda pair, where: (0, pair + offset))


def narrow(length, offset=0):
    return pl.BlockSpec((1, length, 2), lambda pair, where: (pair + offset, 0, 0))


def attention_forward(places, qkvz, decay, slot, before=None):
    length = qkvz.shape[0]
    half = length // 2
    pairs = decay.shape[0]
    rows = pl.BlockSpec((half, LANES), lambda pair, where: (slot, pair))
    column = pl.BlockSpec((1, half, 2), lambda pair, where: (pair, slot, 0))
    held = () if before is None else tuple(before)
    return pl.pallas_call(
        lambda *refs: forward_kernel(slot, *refs),
        grid_spec=pltpu.PrefetchScalarGridSpec(
            num_scalar_prefetch=1,
            grid=(pairs,),
            in_specs=[wide(length, 4 * LANES), narrow(length)]
            + [pl.BlockSpec(memory_space=pl.ANY)] * len(held),
            out_specs=[rows, rows, column],
            scratch_shapes=[pltpu.VMEM((half, LANES), jnp.bfloat16)] * 2
            + [pltpu.VMEM((length, LANES), jnp.bfloat16)],
        ),
        out_shape=[
            jax.ShapeDtypeStruct((length, pairs * LANES), jnp.bfloat16),
            jax.ShapeDtypeStruct((length, pairs * LANES), jnp.float32),
            jax.ShapeDtypeStruct((pairs, length, 2), jnp.float32),
        ],
        input_output_aliases={3 + k: k for k in range(len(held))},
        compiler_params=pltpu.CompilerParams(vmem_limit_bytes=56 << 20),
        cost_estimate=pl.CostEstimate(
            flops=1_000_000, bytes_accessed=1_000_000, transcendentals=0
        ),
        name="attention_forward",
    )(places, qkvz, decay, *held)


def attention_backward(places, qkvz, grad_mixed, attended, decay, log_total, start, count):
    length = qkvz.shape[0]
    return pl.pallas_call(
        backward_kernel,
        grid_spec=pltpu.PrefetchScalarGridSpec(
            num_scalar_prefetch=1,
            grid=(count,),
            in_specs=[wide(length, 4 * LANES, start)]
            + [wide(length, LANES, start)] * 2
            + [narrow(length, start)] * 2,
            out_specs=[wide(length, 4 * LANES), narrow(length)],
            scratch_shapes=[pltpu.VMEM((length, LANES), jnp.bfloat16)] * 5
            + [pltpu.VMEM((length, LANES), jnp.float32)] * 3,
        ),
        out_shape=[
            jax.ShapeDtypeStruct((length, count * 4 * LANES), jnp.bfloat16),
            jax.ShapeDtypeStruct((count, length, 2), jnp.float32),
        ],
        compiler_params=pltpu.CompilerParams(vmem_limit_bytes=56 << 20),
        cost_estimate=pl.CostEstimate(
            flops=7_000_000_000, bytes_accessed=10_000_000, transcendentals=0
        ),
        name="attention_backward",
    )(places, qkvz, grad_mixed, attended, decay, log_total)


def weight_term(left, right):
    return lax.dot_general(
        left, right, (((0,), (0,)), ((), ())), preferred_element_type=jnp.float32
    )


def rms_rows(rows, gain):
    inverse = lax.rsqrt(jnp.mean(rows * rows, axis=-1, keepdims=True) + epsilon)
    return (inverse, rows * inverse * gain)


def rms_back(rows, inverse, gain, grad):
    scaled = grad * gain
    gain_term = jnp.sum(grad * rows * inverse, axis=0)
    row_term = inverse * scaled - rows * inverse**3 * jnp.mean(
        scaled * rows, axis=-1, keepdims=True
    )
    return (row_term, gain_term)


def tie(*values):
    return lax.optimization_barrier(values)


def swap(rows):
    return lax.ppermute(rows, "tensor", [(0, 1), (1, 0)])


def two_devices():
    return lax.axis_size("tensor") == 2


def gather_rows(rows, other=None):
    if not two_devices():
        return lax.all_gather(rows, "tensor", axis=0, tiled=True)
    return jnp.concatenate([rows, swap(rows) if other is None else other], axis=0)


def half_starts(length):
    if not two_devices():
        return jnp.array(0, jnp.int32), jnp.array(length // 2, jnp.int32)
    first = lax.axis_index("tensor") * (length // 2)
    return first, length // 2 - first


class Line:
    def __init__(self):
        self.token = jnp.zeros((), jnp.float32)

    def start(self, values):
        self.token, values = tie(self.token, values)
        return values

    def run(self, step, *values):
        return self.start(step(*self.start(values)))


def scatter_rows(line, product, values, length):
    if not two_devices():
        term = line.run(lambda *v: product(0, length, *v).astype(jnp.bfloat16), *values)
        return lax.psum_scatter(term, "tensor", scatter_dimension=0, tiled=True), jnp.zeros(
            (), jnp.bfloat16
        )
    terms = line.run(lambda *v: product(0, length, *v), *values)
    sent = line.run(lambda t: t[length // 2 :].astype(jnp.bfloat16), terms)
    return terms[: length // 2], swap(sent)


def halves_kernel(mine_ref, left_ref, right_ref, kept_ref, sent_ref, total):
    total[...] = dot_tn(left_ref[...], right_ref[...])
    count, rows, _ = kept_ref.shape
    mine = mine_ref[0]
    for pair in range(count):
        for ref, place in ((kept_ref, mine), (sent_ref, 1 - mine)):
            start = pl.multiple_of((2 * pair + place) * rows, 8)
            ref[pair] = total[pl.ds(start, rows), :].astype(ref.dtype)


def weight_halves(left, right, size):
    length, rows = left.shape
    columns = right.shape[1]
    step = 384
    block = rows // size
    assert rows % step == 0 and step % (2 * block) == 0
    count = step // (2 * block)
    mine = (lax.axis_index("dp") % 2).reshape(1)
    half = pl.BlockSpec((count, block, columns), lambda i, mine: (i, 0, 0))
    return pl.pallas_call(
        halves_kernel,
        grid_spec=pltpu.PrefetchScalarGridSpec(
            num_scalar_prefetch=1,
            grid=(rows // step,),
            in_specs=[
                pl.BlockSpec((length, step), lambda i, mine: (0, i)),
                pl.BlockSpec((length, columns), lambda i, mine: (0, 0)),
            ],
            out_specs=[half, half],
            scratch_shapes=[pltpu.VMEM((step, columns), jnp.float32)],
        ),
        out_shape=[jax.ShapeDtypeStruct((size // 2, block, columns), jnp.bfloat16)] * 2,
        compiler_params=pltpu.CompilerParams(vmem_limit_bytes=40 << 20),
        cost_estimate=pl.CostEstimate(flops=1_000_000, bytes_accessed=1_000_000, transcendentals=0),
        name="weight_halves",
    )(mine, left, right)


def halve_kernel(mine_ref, kept_a, sent_a, kept_b, sent_b, kept_ref, sent_ref):
    kept = kept_a[...].astype(jnp.float32) + kept_b[...].astype(jnp.float32)
    sent = sent_a[...].astype(jnp.float32) + sent_b[...].astype(jnp.float32)
    kept_ref[...] = kept.astype(kept_ref.dtype)
    sent_ref[...] = sent.astype(sent_ref.dtype)


def halve(one, two, axis, mine):
    lead, (rows, columns) = one.shape[:-2], one.shape[-2:]
    before = 2**axis
    after = 2 ** (len(lead) - axis - 1)
    cut = (before, 2, after, rows, columns)
    block = (1, pl.squeezed, 1, rows, columns)
    kept = pl.BlockSpec(block, lambda p, q, mine: (p, mine[0], q, 0, 0))
    sent = pl.BlockSpec(block, lambda p, q, mine: (p, 1 - mine[0], q, 0, 0))
    out = pl.BlockSpec((1, 1, rows, columns), lambda p, q, mine: (p, q, 0, 0))
    one, two = one.reshape(cut), two.reshape(cut)
    parts = pl.pallas_call(
        halve_kernel,
        grid_spec=pltpu.PrefetchScalarGridSpec(
            num_scalar_prefetch=1,
            grid=(before, after),
            in_specs=[kept, sent, kept, sent],
            out_specs=[out, out],
        ),
        out_shape=[jax.ShapeDtypeStruct((before, after, rows, columns), one.dtype)] * 2,
        compiler_params=pltpu.CompilerParams(vmem_limit_bytes=40 << 20),
        cost_estimate=pl.CostEstimate(flops=1_000_000, bytes_accessed=1_000_000, transcendentals=0),
        name="halve",
    )(mine.reshape(1), one, one, two, two)
    shape = lead[:axis] + lead[axis + 1 :] + (rows, columns)
    return [part.reshape(shape) for part in parts]


class WeightSum:
    def __init__(self, line, left, right, masks):
        self.line = line
        self.size = lax.axis_size("dp")
        self.bits = self.size.bit_length() - 1
        kept, sent = line.run(lambda *v: weight_halves(*v, self.size), left, right)
        shape = (2,) * (self.bits - 1) + kept.shape[1:]
        assert masks[0] == 1
        self.masks = list(masks[1:])
        self.left = list(range(self.bits - 1, 0, -1))
        self.terms = [kept.reshape(shape), self.exchange(sent.reshape(shape), 1)]

    def exchange(self, sent, mask):
        return lax.ppermute(sent, "dp", [(i, i ^ mask) for i in range(self.size)])

    def arrive(self):
        self.terms[-1] = self.line.start(self.terms[-1])

    def step(self):
        if not self.masks:
            return
        mask = self.masks.pop(0)
        axis = self.left.index(mask.bit_length() - 1)
        self.left.remove(mask.bit_length() - 1)
        mine = (lax.axis_index("dp") // mask) % 2
        kept, sent = self.line.run(lambda *t: halve(*t, axis, mine), *self.terms)
        self.terms = [kept, self.exchange(sent, mask)]

    def result(self, finish=lambda total: total):
        while self.masks:
            self.step()
        return self.line.run(
            lambda *terms: finish(sum(term.astype(jnp.float32) for term in terms)), *self.terms
        )


class AllSum:
    def __init__(self, line, value, rows):
        self.line, self.value, self.rows, self.mask = line, value, rows, 1
        self.arrived = jnp.zeros((), value.dtype)
        self.step()

    def step(self):
        size = lax.axis_size("dp")
        if self.mask < size:
            mask = self.mask
            self.value = self.line.run(lambda a, b: a + b, self.value, self.arrived)
            self.arrived = lax.ppermute(self.value, "dp", [(i, i ^ mask) for i in range(size)])
            self.mask *= 2

    def result(self):
        while self.mask < lax.axis_size("dp"):
            self.step()
        value = self.line.run(lambda a, b: a + b, self.value, self.arrived)
        top = value[: self.rows]
        if not two_devices():
            return lax.psum(top, "tensor"), value[self.rows :]
        return self.line.run(lambda a, b: a + b, top, swap(top)), value[self.rows :]


def pair_columns(weights, pairs):
    width = pairs * LANES
    padded = [jnp.pad(w, ((0, 0), (0, width - w.shape[1]))) for w in weights]
    parts = [w[:, p * LANES : (p + 1) * LANES] for p in range(pairs) for w in padded]
    return jnp.concatenate(parts, axis=1)


def running_sum(order, values):
    high = lax.reduce_precision(values, 8, 7)
    middle = lax.reduce_precision(values - high, 8, 7)
    terms = jnp.concatenate([high, middle, values - high - middle], axis=1).astype(jnp.bfloat16)
    sums = dot_nn(order, terms)
    return sum(jnp.split(sums, 3, axis=1))


def by_pairs(columns):
    length, heads = columns.shape
    columns = jnp.pad(columns, ((0, 0), (0, heads % 2)))
    return columns.reshape(length, -1, 2).transpose(1, 0, 2)


def from_pairs(pairs, heads):
    return pairs.transpose(1, 0, 2).reshape(pairs.shape[1], -1)[:, :heads]


def local(
    tokens_in,
    prefix_len,
    attn_gain,
    query_weight,
    key_weight,
    value_weight,
    forget_weight,
    forget_bias,
    outgate_weight,
    output_weight,
    mlp_gain,
    gate_weight,
    up_weight,
    down_weight,
    out_grad,
):
    heads_here = forget_weight.shape[1]
    assert prefix_len.shape[0] == 1
    pairs = (heads_here + 1) // 2
    width = heads_here * HD
    first, second = half_starts(LEN)
    places = jnp.stack([prefix_len[0], first, second])
    index = jnp.arange(LEN, dtype=jnp.int32)
    position = (index + first) % LEN
    earlier = (position[None, :] <= position[:, None]).astype(jnp.bfloat16)
    later = (position[None, :] >= position[:, None]).astype(jnp.bfloat16)
    bits = lax.axis_size("dp").bit_length() - 1
    near = [1 << bit for bit in range(bits)]
    far = near[:1] + near[2:] + near[1:2]

    scale_one, normed_rows = rms_rows(tokens_in, attn_gain)
    normed = gather_rows(normed_rows.astype(jnp.bfloat16))
    projection = pair_columns((query_weight, key_weight, value_weight, outgate_weight), pairs)
    output_padded = jnp.pad(output_weight, ((0, pairs * LANES - width), (0, 0)))
    normed, branch_rows = tie(normed, out_grad.astype(jnp.bfloat16))
    grad_branch = gather_rows(branch_rows)
    qkvz = dot_nn(normed, projection).astype(jnp.bfloat16)
    forget_logit = dot_nn(normed, forget_weight) + forget_bias
    decay = by_pairs(running_sum(earlier, jax.nn.log_sigmoid(forget_logit)))
    line = Line()
    saved = line.run(lambda d, q: attention_forward(places, q, d, 1), decay, qkvz)
    grad_branch = line.start(grad_branch)
    half = LEN // 2
    if two_devices():
        sent = line.run(
            lambda m: dot_nn(m[half:], output_padded).astype(jnp.bfloat16), saved[0]
        )
        arrived = swap(sent)
    saved = line.run(lambda d, q, *b: attention_forward(places, q, d, 0, b), decay, qkvz, *saved)
    mixed, attended, log_total = saved
    if two_devices():
        own = line.run(lambda m: dot_nn(m[:half], output_padded), mixed)
    else:
        own, arrived = scatter_rows(
            line, lambda a, b, m, w: dot_nn(m[a:b], w), (mixed, output_padded), LEN
        )
    hidden_rows = tokens_in + line.run(lambda a, b: a + b, own, arrived)

    scale_two, normed_two_rows = rms_rows(hidden_rows, mlp_gain)
    normed_two = gather_rows(line.start(normed_two_rows.astype(jnp.bfloat16)))
    grad_active = line.run(
        lambda g, w: dot_nt(g, w).astype(jnp.bfloat16), grad_branch, down_weight
    )

    def gated(normed_two, grad_active):
        gate = dot_nn(normed_two, gate_weight)
        upward = dot_nn(normed_two, up_weight)
        active = (jax.nn.silu(gate) * upward).astype(jnp.bfloat16)
        gate_sigmoid = jax.nn.sigmoid(gate)
        grad_act_f = grad_active.astype(jnp.float32)
        grad_gate = (
            grad_act_f * upward * gate_sigmoid * (1.0 + gate * (1.0 - gate_sigmoid))
        ).astype(jnp.bfloat16)
        grad_upward = (grad_act_f * gate * gate_sigmoid).astype(jnp.bfloat16)
        return active, grad_gate, grad_upward

    active, grad_gate, grad_upward = line.run(gated, normed_two, grad_active)
    own, arrived = scatter_rows(
        line,
        lambda a, b, g, u: dot_nt(g[a:b], gate_weight) + dot_nt(u[a:b], up_weight),
        (grad_gate, grad_upward),
        LEN,
    )
    down = WeightSum(line, grad_branch, active, near)
    gate_sum = WeightSum(line, normed_two, grad_gate, near)
    up_sum = WeightSum(line, normed_two, grad_upward, near)

    def middle_grads(own, arrived):
        grad_hidden, mlp_gain_part = rms_back(hidden_rows, scale_two, mlp_gain, own + arrived)
        grad_hidden = grad_hidden + out_grad
        return grad_hidden, mlp_gain_part, grad_hidden.astype(jnp.bfloat16)

    grad_hidden, mlp_gain_part, mid_rows = line.run(middle_grads, own, arrived)
    grad_mid = gather_rows(mid_rows)
    down.step()
    last_own, last_arrived = scatter_rows(
        line, lambda a, b, m, w: dot_nn(m[a:b], w), (active, down_weight), LEN
    )
    gate_sum.step()
    up_sum.step()

    grad_mid, grad_mixed = line.run(
        lambda m, w: (m, dot_nt(m, w).astype(jnp.bfloat16)), grad_mid, output_padded
    )
    down.step()
    cut = pairs // 2
    saved = (attended, decay, log_total)
    output_sum = WeightSum(line, grad_mid, mixed[:, :width], far)
    grads_a, decay_a = line.run(
        lambda g: attention_backward(places, qkvz, g, *saved, 0, cut), grad_mixed
    )
    last_arrived = line.start(last_arrived)
    gate_sum.step()
    down.step()
    output_sum.step()
    sum_a = WeightSum(line, normed, grads_a, near)
    grads_b, decay_b = line.run(
        lambda g: attention_backward(places, qkvz, g, *saved, cut, pairs - cut), grad_mixed
    )
    sum_a.step()
    sum_b = WeightSum(line, normed, grads_b, near)
    up_sum.step()
    down.arrive()
    gate_sum.step()
    output_sum.step()
    middle = cut * 4 * LANES

    def forget_term(decay_a, decay_b):
        grad_decay = from_pairs(jnp.concatenate([decay_a, decay_b], axis=0), heads_here)
        return (running_sum(later, grad_decay) * jax.nn.sigmoid(-forget_logit)).astype(
            jnp.bfloat16
        )

    def normed_term(a, b, grads_a, grads_b, grad_forget):
        term = dot_nt(grads_a[a:b], projection[:, :middle])
        term = term + dot_nt(grads_b[a:b], projection[:, middle:])
        return term + dot_nt(grad_forget[a:b], forget_weight)

    grad_forget = line.run(forget_term, decay_a, decay_b)
    sum_a.step()
    up_sum.arrive()
    values = (grads_a, grads_b, grad_forget)
    if two_devices():
        sent = line.run(lambda *v: normed_term(half, LEN, *v).astype(jnp.bfloat16), *values)
        arrived = swap(sent)
    sum_b.step()
    gate_sum.arrive()
    if two_devices():
        own = line.run(lambda *v: normed_term(0, half, *v), *values)
    else:
        own, arrived = scatter_rows(line, normed_term, values, LEN)

    up_sum.step()
    output_sum.arrive()

    def small_terms(grad_forget, normed):
        bias_part = jnp.sum(grad_forget.astype(jnp.float32), axis=0)
        bias_row = lax.dynamic_update_slice_in_dim(
            jnp.zeros((normed.shape[1],), jnp.float32),
            bias_part,
            lax.axis_index("tensor") * heads_here,
            0,
        )
        return bias_row, weight_term(grad_forget, normed)

    bias_row, forget_part = line.run(small_terms, grad_forget, normed)
    sum_a.step()

    def input_grads(own, arrived):
        input_part, attn_gain_part = rms_back(tokens_in, scale_one, attn_gain, own + arrived)
        return grad_hidden + input_part, attn_gain_part

    sum_b.arrive()
    input_grad, attn_gain_part = line.run(input_grads, own, arrived)
    small = jnp.concatenate(
        [jnp.stack([attn_gain_part, mlp_gain_part, bias_row]), forget_part], axis=0
    )
    gains = AllSum(line, small, 3)
    sum_b.step()
    gains.step()
    up_sum.arrive()
    output_sum.step()
    sum_a.arrive()
    down_grad = down.result(jnp.transpose)
    gate_grad = gate_sum.result()
    layer_out = line.run(lambda a, b: hidden_rows + (a + b), last_own, last_arrived)
    gains.step()
    sum_b.step()
    gains.step()
    output_grad = output_sum.result(jnp.transpose)
    up_grad = up_sum.result()
    top, forget_full = gains.result()
    block_rows = forget_full.shape[1] // lax.axis_size("dp")
    forget_grad = lax.dynamic_slice_in_dim(
        forget_full, lax.axis_index("dp") * block_rows, block_rows, 1
    ).T
    block = jnp.concatenate([sum_a.result(), sum_b.result()], axis=1)
    block = block.reshape(block.shape[0], pairs, 4, LANES)
    query_grad, key_grad, value_grad, outgate_grad = [
        block[:, :, part].reshape(block.shape[0], pairs * LANES)[:, :width] for part in range(4)
    ]
    attn_gain_grad, mlp_gain_grad, bias_grad = top[0] + line.token, top[1], top[2, :H]
    return (
        layer_out,
        input_grad,
        attn_gain_grad,
        query_grad,
        key_grad,
        value_grad,
        forget_grad,
        bias_grad,
        outgate_grad,
        output_grad,
        mlp_gain_grad,
        gate_grad,
        up_grad,
        down_grad,
    )


def solution(mesh):
    in_specs = (
        P(("dp", "tensor"), None),
        P("dp"),
        P(),
        P(None, "tensor"),
        P(None, "tensor"),
        P(None, "tensor"),
        P(None, "tensor"),
        P("tensor"),
        P(None, "tensor"),
        P("tensor", None),
        P(),
        P(None, "tensor"),
        P(None, "tensor"),
        P("tensor", None),
        P(("dp", "tensor"), None),
    )
    out_specs = (
        P(("dp", "tensor"), None),
        P(("dp", "tensor"), None),
        P(),
        P("dp", "tensor"),
        P("dp", "tensor"),
        P("dp", "tensor"),
        P("dp", "tensor"),
        P(),
        P("dp", "tensor"),
        P("tensor", "dp"),
        P(),
        P("dp", "tensor"),
        P("dp", "tensor"),
        P("tensor", "dp"),
    )
    return jax.shard_map(local, mesh=mesh, in_specs=in_specs, out_specs=out_specs, check_vma=False)
```
